512 devices in a mesh: exp: 16 (over y, z_hi), skyx: 8 (over z_lo, core), skyy: 4 (over x).
Axes of the slice: x: 4, y: 8, z: 8 (z_hi: 2, z_lo: 4; z = z_hi * 4 + z_lo), core: 2. Of those that a mesh axis runs over, the one named last changes fastest.
Arguments:
- estimate: float32 [2048, 1024], P('skyx', 'skyy'), may hold values from 0.5 to 102
- observed: float32 [16, 2048, 1024], P('exp', 'skyx', 'skyy'), may hold values from 0.25 to 4
- psf_bank: float32 [16, 4, 65, 65], P('exp'), may hold values from 0.1 to 1
- psf_index: int32 [16, 8, 4], P('exp'), may hold values from 0 to 3
- coverage: int32 [16, 8, 4], replicated, may hold values from 0 to 1, as said below
Outputs:
- updated: float32 [2048, 1024], P('skyx', 'skyy')
The draws below stay inside these ranges and needn't reach their ends.
Inputs may be any that keep to these rules, and one draw needn't show every extreme that they name: `coverage`: every tile is covered by at least one exposure.
All inputs are finite; a program needn't handle non-finite values.
Results may differ from the reference program's by a relative error of at most 0.0003.
Values sent between devices are 32-bit elements; how exact they have to be, the bound alone decides.
No kernel may reach another device: no remote copies, remote signals or barrier semaphores. Data moves between devices by JAX's collectives and lax.ppermute only.
A program may use at most 64 MiB of HBM per device.

```python
import math
import jax
import jax.numpy as jnp
from jax import lax

TILE = 256
RADIUS = 32
PSFS = 4
PSF_SIDE = 65
REGION = 320
SPAN = 384
EXPOSURES = 16
TILES_X = 8
TILES_Y = 4
NX = 2048
NY = 1024


def draw_coverage(key, part):
    table_shape = (EXPOSURES, TILES_X, TILES_Y)
    random_bits = jax.random.randint(jax.random.fold_in(key, 11), table_shape, 0, 2)
    leader = jax.random.randint(jax.random.fold_in(key, 12), (TILES_X, TILES_Y), 0, EXPOSURES)
    exposure_rows = lax.broadcasted_iota(jnp.int32, table_shape, 0)
    forced = (exposure_rows == leader[None]).astype(jnp.int32)
    return jnp.maximum(random_bits, forced).astype(jnp.int32)


def draw_estimate(key, part):
    grid_shape = (NX, NY)
    lit_mask = jax.random.randint(jax.random.fold_in(key, 21), grid_shape, 0, 256) == 0
    spread = jax.random.uniform(jax.random.fold_in(key, 22), grid_shape, jnp.float32)
    levels = jax.random.uniform(jax.random.fold_in(key, 23), grid_shape, jnp.float32)
    background = jnp.exp(jnp.log(0.5) + jnp.log(4.0) * spread)
    flux_values = jnp.exp(jnp.log(0.1) + jnp.log(1000.0) * levels)
    return (background + jnp.where(lit_mask, flux_values, 0.0)).astype(jnp.float32)


def plant(entries, stream_key, least, high):
    shape = entries.shape
    place = [jax.random.randint(jax.random.fold_in(stream_key, axis), (), 0, shape[axis]) for axis in range(len(shape))]
    entries = entries.at[tuple(place)].set(least)
    longest = shape.index(max(shape))
    place[longest] = (place[longest] + 1) % shape[longest]
    return entries.at[tuple(place)].set(high)


def level_of(own_key, dims, pieces, least, largest):
    def one(position, blocks):
        heights = jax.random.uniform(jax.random.fold_in(jax.random.fold_in(own_key, 6), position), (blocks,), jnp.float32, least / len(pieces), largest / len(pieces))
        return jnp.repeat(jnp.exp(heights), dims[position] // blocks).reshape((-1,) + (1,) * (len(dims) - position - 1))

    loudness = one(*pieces[0])
    for cut in pieces[1:]:
        loudness = loudness * one(*cut)
    return loudness


def setup_inputs(seed: int = 0) -> dict:
    splits = jax.random.split(jax.random.key(seed), 6)
    return {
        "estimate": draw_estimate(jax.random.fold_in(splits[5], 71), 0),
        "observed": jnp.clip(jnp.exp(math.log(4.0) - 2.7725887 * jax.random.uniform(splits[1], (EXPOSURES, NX, NY), jnp.float32) ** level_of(splits[1], (EXPOSURES, NX, NY), ((0, 16), (1, 8), (2, 4)), -0.2, 0.2)), 0.25, 4.0),
        "psf_bank": jnp.clip(jnp.exp(math.log(1.0) - 2.3025851 * jax.random.uniform(splits[2], (EXPOSURES, PSFS, PSF_SIDE, PSF_SIDE), jnp.float32) ** level_of(splits[2], (EXPOSURES, PSFS, PSF_SIDE, PSF_SIDE), ((0, 16),), -0.2, 0.2)), 0.1, 1.0),
        "psf_index": plant(jax.random.randint(splits[3], (EXPOSURES, TILES_X, TILES_Y), 0, PSFS), jax.random.fold_in(splits[3], 1), 0, PSFS - 1).astype(jnp.int32),
        "coverage": draw_coverage(jax.random.fold_in(splits[5], 71), 0),
    }


def envelope_kernels(psf_bank):
    offsets = jnp.arange(PSF_SIDE, dtype=jnp.float32) - RADIUS
    envelope = jnp.exp(-(offsets[:, None] ** 2 + offsets[None, :] ** 2) / (2.0 * (0.625 * RADIUS) ** 2))
    raw = psf_bank * envelope
    return raw / jnp.sum(raw, axis=(2, 3), keepdims=True)


def to_sky(blocks):
    return blocks.reshape(TILES_X, TILES_Y, TILE, TILE).transpose(0, 2, 1, 3).reshape(NX, NY)


def forward(window, kernel):
    spectrum = jnp.fft.fft2(window, s=(SPAN, SPAN)) * jnp.fft.fft2(kernel, s=(SPAN, SPAN))
    return jnp.real(jnp.fft.ifft2(spectrum))[2 * RADIUS:2 * RADIUS + TILE, 2 * RADIUS:2 * RADIUS + TILE]


def adjoint(window, kernel):
    spectrum = jnp.fft.fft2(window, s=(SPAN, SPAN)) * jnp.conj(jnp.fft.fft2(kernel, s=(SPAN, SPAN)))
    return jnp.real(jnp.fft.ifft2(spectrum))[:TILE, :TILE]


def tile_map(method, padded, tile_kernels):
    flat = tile_kernels.reshape(TILES_X * TILES_Y, PSF_SIDE, PSF_SIDE)

    def single(packed):
        number, kernel = packed
        row_start = (number // TILES_Y) * TILE
        col_start = (number % TILES_Y) * TILE
        window = lax.dynamic_slice(padded, (row_start, col_start), (REGION, REGION))
        return method(window, kernel)

    numbers = jnp.arange(TILES_X * TILES_Y, dtype=jnp.int32)
    return to_sky(lax.map(single, (numbers, flat)))


def reference(estimate, observed, psf_bank, psf_index, coverage):
    kernels_all = envelope_kernels(psf_bank)
    padded = jnp.pad(estimate, RADIUS)

    def per_exposure(total, packed):
        frames, kernels, chosen, cover = packed
        tile_kernels = kernels[chosen]
        blurred = tile_map(forward, padded, tile_kernels)
        mask = jnp.repeat(jnp.repeat(cover.astype(jnp.float32), TILE, 0), TILE, 1)
        ratio = mask * frames / blurred
        back = mask * tile_map(adjoint, jnp.pad(ratio, RADIUS), tile_kernels)
        return total + back, None

    start = jnp.zeros((NX, NY), jnp.float32)
    total = lax.scan(per_exposure, start, (observed, kernels_all, psf_index, coverage))[0]
    covering = jnp.repeat(jnp.repeat(jnp.sum(coverage, 0).astype(jnp.float32), TILE, 0), TILE, 1)
    return estimate * total / covering
```

```python
import jax
import jax.numpy as jnp
from jax import lax
from jax.sharding import Mesh
from jax.sharding import PartitionSpec as P

precise_mode = lax.Precision.HIGHEST


def with_halo(block, sides, width):
    for axis, dim in sides:
        count = lax.axis_size(axis)
        forward = [(i, i + 1) for i in range(count - 1)]
        backward = [(target, source) for source, target in forward]
        low = lax.ppermute(
            lax.slice_in_dim(block, block.shape[dim] - width, None, axis=dim), axis, forward
        )
        high = lax.ppermute(lax.slice_in_dim(block, 0, width, axis=dim), axis, backward)
        block = jnp.concatenate([low, block, high], axis=dim)
    return block


def product(left_side, right_side):
    return jnp.dot(
        left_side, right_side, precision=precise_mode, preferred_element_type=jnp.float32
    )


def tables(row_count, offset, length):
    places = jnp.arange(row_count, dtype=jnp.int32) + offset
    frequency = jnp.arange(length, dtype=jnp.int32)
    phases = places[:, None] * frequency[None, :] % length
    angles = phases.astype(jnp.float32) * (2.0 * jnp.pi / length)
    return (jnp.cos(angles), jnp.sin(angles))


def transform(source_field, cos_in, sin_in):
    rows_re = product(source_field, cos_in)
    rows_im = -product(source_field, sin_in)
    spec_re = product(cos_in.T, rows_re) + product(sin_in.T, rows_im)
    spec_im = product(cos_in.T, rows_im) - product(sin_in.T, rows_re)
    return (spec_re, spec_im)


def inverse(spec_re, spec_im, cos_rows, sin_rows, cos_cols, sin_cols):
    left_re = product(cos_rows, spec_re) - product(sin_rows, spec_im)
    left_im = product(cos_rows, spec_im) + product(sin_rows, spec_re)
    length = cos_rows.shape[1]
    return (product(left_re, cos_cols.T) - product(left_im, sin_cols.T)) / (length * length)


def tile_entry(lookup, row_pick, col_pick):
    rows_hit = jnp.arange(lookup.shape[-2], dtype=jnp.int32) == row_pick
    cols_hit = jnp.arange(lookup.shape[-1], dtype=jnp.int32) == col_pick
    hit_mask = (rows_hit[:, None] & cols_hit[None, :]).astype(jnp.int32)
    return jnp.sum(lookup * hit_mask, axis=(-2, -1))


def kernel_spectrum(bank_row, envelope, cos_part, sin_part):
    raw_kernel = bank_row * envelope
    return transform(raw_kernel / jnp.sum(raw_kernel), cos_part, sin_part)


def exposure_sum(block):
    rows, cols = block.shape
    near = lax.axis_size("exp_y")
    pieces = lax.all_to_all(block.reshape(near, rows // near, cols), "exp_y", 0, 0)
    piece = jnp.sum(pieces, axis=0)
    piece = piece + lax.ppermute(piece, "exp_z", [(0, 1), (1, 0)])
    spread = jnp.broadcast_to(piece[None], (near,) + piece.shape)
    return lax.all_to_all(spread, "exp_y", 0, 0).reshape(rows, cols)


def shards(estimate, observed, psf_bank, psf_index, coverage):
    tile_side = estimate.shape[0]
    psf_side = psf_bank.shape[-1]
    model_count = psf_bank.shape[1]
    radius = (psf_side - 1) // 2
    region = tile_side + 2 * radius
    dft_len = tile_side + 4 * radius
    offsets = jnp.arange(psf_side, dtype=jnp.float32) - radius
    envelope = jnp.exp(
        -(offsets[:, None] ** 2 + offsets[None, :] ** 2) / (2.0 * (0.625 * radius) ** 2)
    )
    count_here = observed.shape[0]
    first_exp = lax.axis_index(("exp_y", "exp_z")) * count_here
    tile_row = lax.axis_index("skyx")
    tile_col = lax.axis_index("skyy")
    cover_own = tile_entry(coverage, tile_row, tile_col).astype(jnp.float32)
    covering = jnp.sum(cover_own)
    mine_cover = lax.dynamic_slice_in_dim(cover_own, first_exp, count_here)
    own_models = tile_entry(psf_index, tile_row, tile_col)
    models = jnp.arange(model_count, dtype=jnp.int32)
    cos_in, sin_in = tables(region, 0, dft_len)
    cos_adj, sin_adj = tables(tile_side, 0, dft_len)
    cos_fwd, sin_fwd = tables(tile_side, 2 * radius, dft_len)
    padded = with_halo(estimate, (("skyx", 0), ("skyy", 1)), radius)
    image_re, image_im = transform(padded, cos_in, sin_in)
    member = 0
    picked = (models == own_models[member]).astype(jnp.float32)
    chosen_raw = jnp.sum(picked[:, None, None] * psf_bank[member], axis=0)
    kern_re, kern_im = kernel_spectrum(chosen_raw, envelope, cos_in[:psf_side], sin_in[:psf_side])
    blurred = inverse(
        image_re * kern_re - image_im * kern_im,
        image_re * kern_im + image_im * kern_re,
        cos_fwd,
        sin_fwd,
        cos_fwd,
        sin_fwd,
    )
    ratios = [mine_cover[member] * observed[member] / blurred]
    spectra = [(kern_re, kern_im)]
    ratio_fields = with_halo(jnp.stack(ratios), (("skyx", 1), ("skyy", 2)), radius)
    member = 0
    ratio_re, ratio_im = transform(ratio_fields[member], cos_in, sin_in)
    kern_re, kern_im = spectra[member]
    back_proj = inverse(
        ratio_re * kern_re + ratio_im * kern_im,
        ratio_im * kern_re - ratio_re * kern_im,
        cos_adj,
        sin_adj,
        cos_adj,
        sin_adj,
    )
    summed_back = mine_cover[member] * back_proj
    summed = exposure_sum(summed_back)
    return estimate * summed / covering


def solution(mesh):
    exp_count, sky_rows, sky_cols = mesh.devices.shape
    mesh = Mesh(
        mesh.devices.reshape(exp_count // 2, 2, sky_rows, sky_cols),
        ("exp_y", "exp_z", "skyx", "skyy"),
    )
    exp = ("exp_y", "exp_z")
    in_specs = (
        P("skyx", "skyy"),
        P(exp, "skyx", "skyy"),
        P(exp, None, None, None),
        P(exp, None, None),
        P(),
    )
    out_specs = P("skyx", "skyy")
    return jax.shard_map(shards, mesh=mesh, in_specs=in_specs, out_specs=out_specs, check_vma=False)
```

```python
import functools

import jax
import jax.numpy as jnp
import numpy as np
from jax import lax
from jax.experimental import pallas as pl
from jax.experimental.pallas import tpu as pltpu
from jax.sharding import Mesh
from jax.sharding import PartitionSpec as P

TILE = 256
RADIUS = 32
SIDE = 2 * RADIUS + 1
MARGIN = 2 * RADIUS
LANES = 128
FRAME = TILE + 2 * MARGIN
HALF = FRAME // 2
BLOCK = 256
MODELS = 4
REACH = TILE + 2 * RADIUS


def halves(table):
    table = np.asarray(table, np.float32)
    high = table.astype(jnp.bfloat16)
    low = (table - high.astype(np.float32)).astype(jnp.bfloat16)
    return high, low


def waves(places, length):
    frequency = np.arange(length // 2, dtype=np.float64) + 0.5
    angle = 2.0 * np.pi / length * frequency[:, None] * np.asarray(places, np.float64)[None, :]
    return np.concatenate([np.cos(angle), np.sin(angle)], axis=0)


@functools.cache
def tables():
    rows = waves(np.arange(FRAME), FRAME)
    column = np.where(np.arange(FRAME) < TILE + MARGIN, np.arange(FRAME), np.arange(FRAME) - FRAME)
    blocks_in = []
    blocks_out = []
    for start in (-MARGIN, TILE // 2 - RADIUS):
        place = column - start
        used = (place >= 0) & (place < BLOCK - RADIUS)
        blocks_in.append((waves(place, BLOCK) * used[None, :]).T)
        own = np.arange(LANES) + (0 if start < 0 else LANES)
        edge = column[TILE:]
        edge_used = (edge >= -RADIUS) & (edge < 0) if start < 0 else (edge < TILE + RADIUS) & (edge > 0)
        own_part = waves(own - start, BLOCK)
        edge_part = waves(edge - start, BLOCK) * edge_used[None, :]
        blocks_out.append(np.concatenate([own_part, edge_part], axis=1))
    col_in = np.concatenate(blocks_in, axis=1)
    col_out = np.concatenate(blocks_out, axis=1)
    offsets = np.arange(LANES) - RADIUS
    inside = offsets <= RADIUS
    kernel_rows = waves(offsets, FRAME) * inside[None, :]
    kernel_cols = (waves(offsets, BLOCK) * inside[None, :]).T

    def across(table):
        high, low = halves(table)
        return np.concatenate([high, high, low], axis=1)

    def down(table):
        high, low = halves(table)
        return np.concatenate([high, high, low], axis=0)

    return {
        "row_in": across(rows),
        "row_out": across(rows.T[RADIUS : FRAME - RADIUS]),
        "col_in": down(col_in),
        "col_out": np.concatenate([down(col_out[:, :BLOCK]), down(col_out[:, BLOCK:])], axis=1),
        "kernel_rows": across(kernel_rows),
        "kernel_cols": down(kernel_cols),
    }


def split(value):
    high = value.astype(jnp.bfloat16)
    low = (value - high.astype(jnp.float32)).astype(jnp.bfloat16)
    return high, low


def matmul(left, right):
    return jnp.dot(left, right, preferred_element_type=jnp.float32)


def put_across(ref, rows, value, first=0):
    high, low = split(value)
    width = value.shape[1]
    ref[rows, first : first + width] = high
    ref[rows, first + width : first + 2 * width] = low
    ref[rows, first + 2 * width : first + 3 * width] = high


def put_down(ref, value, depth, row, cols):
    high, low = split(value)
    count = value.shape[0]
    ref[row : row + count, cols] = high
    ref[depth + row : depth + row + count, cols] = low
    ref[2 * depth + row : 2 * depth + row + count, cols] = high


def spectrum_kernel(bank_ref, rows_ref, cols_ref, out_ref, raw_ref, wide_ref, tall_ref):
    shape = (SIDE, SIDE)
    a = lax.broadcasted_iota(jnp.int32, shape, 0).astype(jnp.float32) - RADIUS
    b = lax.broadcasted_iota(jnp.int32, shape, 1).astype(jnp.float32) - RADIUS
    envelope = jnp.exp(-(a * a + b * b) / (2.0 * (0.625 * RADIUS) ** 2))
    raw_ref[...] = jnp.zeros_like(raw_ref)
    gain = 4.0 / (FRAME * BLOCK)

    def one(model, carry):
        raw = bank_ref[model] * envelope
        total = jnp.sum(jnp.sum(raw, axis=1, keepdims=True), axis=0, keepdims=True)
        raw_ref[0:SIDE, 0:SIDE] = raw / total
        put_across(wide_ref, slice(None), raw_ref[...])
        put_down(tall_ref, matmul(wide_ref[...], cols_ref[...]), LANES, 0, slice(None))
        out_ref[model] = matmul(rows_ref[...], tall_ref[...]) * gain
        return carry

    lax.fori_loop(0, MODELS, one, 0)


def kernel_spectra(bank, table):
    return pl.pallas_call(
        spectrum_kernel,
        out_shape=jax.ShapeDtypeStruct((MODELS, FRAME, BLOCK), jnp.float32),
        in_specs=[pl.BlockSpec(memory_space=pltpu.VMEM)] * 3,
        out_specs=pl.BlockSpec(memory_space=pltpu.VMEM),
        scratch_shapes=[
            pltpu.VMEM((LANES, LANES), jnp.float32),
            pltpu.VMEM((LANES, 3 * LANES), jnp.bfloat16),
            pltpu.VMEM((3 * LANES, BLOCK), jnp.bfloat16),
        ],
        compiler_params=pltpu.CompilerParams(vmem_limit_bytes=8 << 20),
        cost_estimate=pl.CostEstimate(flops=4 << 28, bytes_accessed=4 << 20, transcendentals=8192),
        name="kernel_spectra",
    )(bank, table["kernel_rows"], table["kernel_cols"])


def mixed(spec_ref, kern, block, sign, grown_ref, rows_step=64):
    base = block * BLOCK
    for row in range(0, HALF, rows_step):
        top = slice(row, row + rows_step)
        low = slice(HALF + row, HALF + row + rows_step)
        near = slice(base, base + LANES)
        far = slice(base + LANES, base + BLOCK)
        fa, fb = spec_ref[top, near], spec_ref[top, far]
        fc, fd = spec_ref[low, near], spec_ref[low, far]
        ka, kb = kern[top, 0:LANES], kern[top, LANES:BLOCK]
        kc, kd = kern[low, 0:LANES], kern[low, LANES:BLOCK]
        if sign > 0:
            cc = fa * ka - fb * kb - fc * kc + fd * kd
            cs = fa * kb + fb * ka - fc * kd - fd * kc
            sc = fa * kc + fc * ka - fb * kd - fd * kb
            ss = fa * kd + fd * ka + fb * kc + fc * kb
        else:
            cc = fa * ka + fb * kb + fc * kc + fd * kd
            cs = fb * ka - fa * kb - fc * kd + fd * kc
            sc = fc * ka - fa * kc - fb * kd + fd * kb
            ss = fa * kd + fd * ka - fb * kc - fc * kb
        put_down(grown_ref, cc, FRAME, row, near)
        put_down(grown_ref, cs, FRAME, row, far)
        put_down(grown_ref, sc, FRAME, HALF + row, near)
        put_down(grown_ref, ss, FRAME, HALF + row, far)


def update_kernel(
    place_ref, index_ref, cover_ref,
    est_ref, obs_ref, side_ref, above_ref, below_ref, kern_ref,
    row_in_ref, row_out_ref, col_in_ref, col_out_ref,
    out_ref,
    wide_ref, tall_ref, spec_ref, grown_ref, mid_ref, blur_ref, pick_ref, mask_ref,
):
    member, tile_row, tile_col = place_ref[0], place_ref[1], place_ref[2]
    rows_of_tiles, cols_of_tiles = index_ref.shape[1], index_ref.shape[2]
    exposures = cover_ref.shape[0]

    wide = lambda rows, value: put_across(wide_ref, rows, value)
    wide(slice(0, MARGIN), above_ref[0:MARGIN, :])
    wide(slice(FRAME - MARGIN, FRAME), below_ref[0:MARGIN, :])
    for row in range(0, TILE, 64):
        rows = slice(row, row + 64)
        wide(slice(MARGIN + row, MARGIN + row + 64), jnp.concatenate([est_ref[rows, :], side_ref[rows, 0:LANES]], axis=1))

    lane = lax.broadcasted_iota(jnp.int32, (RADIUS, FRAME), 1)
    for step, first, count in ((-1, 0, RADIUS), (0, RADIUS, TILE), (1, RADIUS + TILE, RADIUS)):
        near = []
        for side in (0, 1, -1):
            r, c = tile_row + step, tile_col + side
            inside = (r >= 0) & (r < rows_of_tiles) & (c >= 0) & (c < cols_of_tiles)
            r = jnp.clip(r, 0, rows_of_tiles - 1)
            c = jnp.clip(c, 0, cols_of_tiles - 1)
            near.append((index_ref[0, r, c], jnp.where(inside, cover_ref[member, r, c], 0)))
        pick = jnp.where(lane < TILE, near[0][0], jnp.where(lane < TILE + RADIUS, near[1][0], near[2][0]))
        cover = jnp.where(
            lane < TILE, near[0][1],
            jnp.where(lane < TILE + RADIUS, near[1][1], jnp.where(lane < FRAME - RADIUS, 0, near[2][1])),
        )
        for row in range(first, first + count, RADIUS):
            pick_ref[row : row + RADIUS, :] = pick
            mask_ref[row : row + RADIUS, :] = cover

    def analyse():
        for row in range(0, FRAME, 128):
            rows = slice(row, row + 128)
            put_down(tall_ref, matmul(wide_ref[rows, :], col_in_ref[...]), FRAME, row, slice(None))
        for row in range(0, FRAME, 128):
            rows = slice(row, row + 128)
            spec_ref[rows, :] = matmul(row_in_ref[rows, :], tall_ref[...])

    analyse()

    def forward(model, carry):
        for block in range(2):
            mixed(spec_ref, kern_ref.at[model], block, 1, grown_ref)
        for row in range(0, REACH, 160):
            rows = slice(row, row + 160)
            part = matmul(row_out_ref[rows, :], grown_ref[...])
            for block in range(2):
                put_across(mid_ref, rows, part[:, block * BLOCK : (block + 1) * BLOCK], block * 3 * BLOCK)
        for row in range(0, REACH, 160):
            rows = slice(row, row + 160)
            sides = []
            for block in range(2):
                part = matmul(
                    mid_ref[rows, block * 3 * BLOCK : (block + 1) * 3 * BLOCK],
                    col_out_ref[:, block * BLOCK : (block + 1) * BLOCK],
                )
                own = slice(block * LANES, (block + 1) * LANES)
                blur_ref[rows, own] = jnp.where(pick_ref[rows, own] == model, part[:, 0:LANES], blur_ref[rows, own])
                sides.append(part[:, LANES:BLOCK])
            edge = slice(TILE, FRAME)
            blur_ref[rows, edge] = jnp.where(pick_ref[rows, edge] == model, sides[0] + sides[1], blur_ref[rows, edge])
        return carry

    lax.fori_loop(0, MODELS, forward, 0)

    def ratio(rows, values):
        return jnp.where(mask_ref[rows, :] != 0, values / blur_ref[rows, :], 0.0)

    wide(slice(0, RADIUS), jnp.zeros((RADIUS, FRAME), jnp.float32))
    wide(slice(FRAME - RADIUS, FRAME), jnp.zeros((RADIUS, FRAME), jnp.float32))
    wide(slice(RADIUS, MARGIN), ratio(slice(0, RADIUS), above_ref[MARGIN : MARGIN + RADIUS, :]))
    wide(
        slice(FRAME - MARGIN, FRAME - RADIUS),
        ratio(slice(RADIUS + TILE, REACH), below_ref[MARGIN : MARGIN + RADIUS, :]),
    )
    for row in range(0, TILE, 64):
        rows = slice(row, row + 64)
        values = jnp.concatenate([obs_ref[rows, :], side_ref[rows, LANES : 2 * LANES]], axis=1)
        wide(slice(MARGIN + row, MARGIN + row + 64), ratio(slice(RADIUS + row, RADIUS + row + 64), values))

    analyse()

    own_model = index_ref[0, tile_row, tile_col]
    for block in range(2):
        mixed(spec_ref, kern_ref.at[own_model], block, -1, grown_ref)

    covering = lax.fori_loop(0, exposures, lambda e, n: n + cover_ref[e, tile_row, tile_col], 0)
    own_cover = cover_ref[member, tile_row, tile_col].astype(jnp.float32)
    weight = jnp.full((1, LANES), own_cover, jnp.float32) / jnp.full((1, LANES), covering.astype(jnp.float32), jnp.float32)
    for row in range(0, TILE, 128):
        rows = slice(row, row + 128)
        part = matmul(row_out_ref[RADIUS + row : RADIUS + row + 128, :], grown_ref[...])
        for block in range(2):
            put_across(mid_ref, rows, part[:, block * BLOCK : (block + 1) * BLOCK], block * 3 * BLOCK)
        for block in range(2):
            back = matmul(
                mid_ref[rows, block * 3 * BLOCK : (block + 1) * 3 * BLOCK],
                col_out_ref[:, block * BLOCK : block * BLOCK + LANES],
            )
            own = slice(block * LANES, (block + 1) * LANES)
            out_ref[rows, own] = est_ref[rows, own] * (back * weight)


def tile_update(place, index, coverage, estimate, observed, side, above, below, spectra, table):
    vmem = pl.BlockSpec(memory_space=pltpu.VMEM)
    smem = pl.BlockSpec(memory_space=pltpu.SMEM)
    return pl.pallas_call(
        update_kernel,
        out_shape=jax.ShapeDtypeStruct((TILE, TILE), jnp.float32),
        in_specs=[smem] * 3 + [vmem] * 10,
        out_specs=vmem,
        scratch_shapes=[
            pltpu.VMEM((FRAME, 3 * FRAME), jnp.bfloat16),
            pltpu.VMEM((3 * FRAME, 2 * BLOCK), jnp.bfloat16),
            pltpu.VMEM((FRAME, 2 * BLOCK), jnp.float32),
            pltpu.VMEM((3 * FRAME, 2 * BLOCK), jnp.bfloat16),
            pltpu.VMEM((REACH, 6 * BLOCK), jnp.bfloat16),
            pltpu.VMEM((REACH, FRAME), jnp.float32),
            pltpu.VMEM((REACH, FRAME), jnp.int32),
            pltpu.VMEM((REACH, FRAME), jnp.int32),
        ],
        compiler_params=pltpu.CompilerParams(vmem_limit_bytes=24 << 20),
        cost_estimate=pl.CostEstimate(flops=5 << 30, bytes_accessed=8 << 20, transcendentals=0),
        name="tile_update",
    )(
        place, index, coverage, estimate, observed, side, above, below, spectra,
        table["row_in"], table["row_out"], table["col_in"], table["col_out"],
    )


def neighbours(axis):
    count = lax.axis_size(axis)
    upward = [(i, i + 1) for i in range(count - 1)]
    return upward, [(b, a) for a, b in upward]


def exchange(first, last, axis):
    upward, downward = neighbours(axis)
    return lax.ppermute(last, axis, upward), lax.ppermute(first, axis, downward)


def exposure_sum(block):
    rows, cols = block.shape
    near = lax.axis_size("exp_y")
    pieces = lax.all_to_all(block.reshape(near, rows // near, cols), "exp_y", 0, 0)
    piece = jnp.sum(pieces, axis=0)
    piece = piece + lax.ppermute(piece, "exp_z", [(0, 1), (1, 0)])
    spread = jnp.broadcast_to(piece[None], (near,) + piece.shape)
    return lax.all_to_all(spread, "exp_y", 0, 0).reshape(rows, cols)


def shards(estimate, observed, psf_bank, psf_index, coverage):
    table = {name: jnp.asarray(value) for name, value in tables().items()}
    frame = observed[0]
    place = jnp.stack(
        [lax.axis_index(("exp_y", "exp_z")), lax.axis_index("skyx"), lax.axis_index("skyy")]
    ).astype(jnp.int32)
    first = jnp.concatenate([estimate[:, :MARGIN], frame[:, :MARGIN]], axis=1)
    last = jnp.concatenate([frame[:, TILE - MARGIN :], estimate[:, TILE - MARGIN :]], axis=1)
    left, right = exchange(first, last, "skyy")
    side = jnp.concatenate(
        [right[:, :MARGIN], left[:, MARGIN:], right[:, MARGIN:], left[:, :MARGIN]], axis=1
    )
    rows_up = jnp.concatenate(
        [
            jnp.concatenate([estimate[:MARGIN], side[:MARGIN, :LANES]], axis=1),
            jnp.concatenate([frame[:RADIUS], side[:RADIUS, LANES:]], axis=1),
        ],
        axis=0,
    )
    rows_down = jnp.concatenate(
        [
            jnp.concatenate([estimate[TILE - MARGIN :], side[TILE - MARGIN :, :LANES]], axis=1),
            jnp.concatenate([frame[TILE - RADIUS :], side[TILE - RADIUS :, LANES:]], axis=1),
        ],
        axis=0,
    )
    above, below = exchange(rows_up, rows_down, "skyx")
    spectra = kernel_spectra(psf_bank[0], table)
    back = tile_update(place, psf_index, coverage, estimate, frame, side, above, below, spectra, table)
    return exposure_sum(back)


def solution(mesh):
    exp_count, sky_rows, sky_cols = mesh.devices.shape
    mesh = Mesh(
        mesh.devices.reshape(exp_count // 2, 2, sky_rows, sky_cols),
        ("exp_y", "exp_z", "skyx", "skyy"),
    )
    exp = ("exp_y", "exp_z")
    in_specs = (
        P("skyx", "skyy"),
        P(exp, "skyx", "skyy"),
        P(exp, None, None, None),
        P(exp, None, None),
        P(),
    )
    return jax.shard_map(
        shards, mesh=mesh, in_specs=in_specs, out_specs=P("skyx", "skyy"), check_vma=False
    )
```

```python
import functools

import jax
import jax.numpy as jnp
import numpy as np
from jax import lax
from jax.experimental import pallas as pl
from jax.experimental.pallas import tpu as pltpu
from jax.sharding import Mesh
from jax.sharding import PartitionSpec as P

TILE = 256
RADIUS = 32
SIDE = 2 * RADIUS + 1
MARGIN = 2 * RADIUS
LANES = 128
FRAME = TILE + 2 * MARGIN
HALF = FRAME // 2
BLOCK = 256
HALO = MARGIN + RADIUS
MODELS = 4
REACH = TILE + 2 * RADIUS
FOLD = REACH // 2
DEPTH = 80
PAIRED = True


def halves(table):
    table = np.asarray(table, np.float32)
    high = table.astype(jnp.bfloat16)
    low = (table - high.astype(np.float32)).astype(jnp.bfloat16)
    return high, low


def waves(places, length):
    frequency = np.arange(length // 2, dtype=np.float64) + 0.5
    angle = 2.0 * np.pi / length * frequency[:, None] * np.asarray(places, np.float64)[None, :]
    return np.concatenate([np.cos(angle), np.sin(angle)], axis=0)


@functools.cache
def tables():
    own = np.arange(MARGIN, HALF) + 0.5
    near = np.arange(RADIUS, MARGIN) + 0.5
    far = np.arange(RADIUS) + 0.5
    margin = np.arange(MARGIN) + 0.5
    starts = (-MARGIN, TILE // 2 - RADIUS)
    column_in = []
    column_out = []
    column_back = []
    for block, start in enumerate(starts):
        column = np.arange(BLOCK) + block * LANES - MARGIN
        place = column - start
        used = (place >= 0) & (place < BLOCK - RADIUS)
        column_in.append((waves(place, BLOCK) * used[None, :]).T)
        first, last = (-RADIUS, LANES) if block == 0 else (LANES, TILE + RADIUS)
        wanted = (column >= first) & (column < last)
        column_out.append(waves(place, BLOCK) * wanted[None, :])
        column_back.append(waves(np.arange(LANES) + block * LANES - start, BLOCK))
    offsets = np.arange(LANES) - RADIUS
    inside = offsets <= RADIUS
    kernel_rows = (waves(offsets, FRAME) * inside[None, :])[:, :DEPTH]
    kernel_cols = (waves(offsets, BLOCK) * inside[None, :]).T

    def across(table):
        high, low = halves(table)
        return np.concatenate([high, high, low], axis=1)

    def pair(table):
        return np.concatenate(halves(table), axis=0)

    def both(places, build=lambda t: t):
        full = waves(places, FRAME)
        return np.concatenate([across(build(full[:HALF])), across(build(full[HALF:]))], axis=0)

    every = np.concatenate([own, near, far])
    ready = np.zeros((FRAME + 3 * BLOCK, BLOCK + 3 * LANES), jnp.bfloat16)
    ready[0:FRAME, 0 : 3 * DEPTH] = across(kernel_rows)
    ready[0:FRAME, BLOCK:] = both(own)
    ready[FRAME : FRAME + 2 * BLOCK, 0 : 2 * BLOCK] = pair(np.concatenate(column_in, axis=1))
    ready[FRAME + 2 * BLOCK :, 0:BLOCK] = pair(kernel_cols)
    return {
        "ready": ready,
        "row_margin": both(margin),
        "row_in": both(every),
        "row_out": both(np.concatenate([own, near]), lambda t: t.T),
        "col_in": pair(np.concatenate(column_in, axis=1)),
        "col_out": pair(np.concatenate(column_out, axis=1)),
        "col_back": pair(np.concatenate(column_back, axis=1)),
    }


def split(value):
    high = value.astype(jnp.bfloat16)
    low = (value - high.astype(jnp.float32)).astype(jnp.bfloat16)
    return high, low


def matmul(left, right):
    return jnp.dot(left, right, preferred_element_type=jnp.float32)


def put_across(ref, rows, value):
    width = value.shape[1]
    ref[rows, 0:width], ref[rows, width : 2 * width] = split(value)


def put_down(ref, row, depth, value, cols=slice(None)):
    count = value.shape[0]
    ref[row : row + count, cols], ref[depth + row : depth + row + count, cols] = split(value)


def across3(ref, rows, first, width, total):
    high = ref[rows, first : first + width]
    return jnp.concatenate([high, ref[rows, total + first : total + first + width], high], axis=1)


def table3(ref, cols=slice(None)):
    depth = ref.shape[0] // 2
    high = ref[0:depth, cols]
    return jnp.concatenate([high, high, ref[depth:, cols]], axis=0)


def data3(ref, first, depth, total, cols=slice(None)):
    high = ref[first : first + depth, cols]
    return jnp.concatenate([high, ref[total + first : total + first + depth, cols], high], axis=0)


def reverse(value):
    count = value.shape[0]
    i = lax.broadcasted_iota(jnp.int32, (count, count), 0)
    j = lax.broadcasted_iota(jnp.int32, (count, count), 1)
    swap = jnp.where(i + j == count - 1, 1.0, 0.0).astype(jnp.bfloat16)
    high, low = split(value)
    return matmul(swap, high) + matmul(swap, low)


def turn(value):
    return pltpu.roll(value, MARGIN, 1)


def low_lanes(rows):
    return lax.broadcasted_iota(jnp.int32, (rows, LANES), 1) < MARGIN


def window_rows(own_ref, left, right, rows):
    low = low_lanes(left.shape[0])
    one, two = turn(own_ref[rows, 0:LANES]), turn(own_ref[rows, LANES:TILE])
    return jnp.concatenate(
        [jnp.where(low, left, one), jnp.where(low, one, two), jnp.where(low, two, right)], axis=1
    )


def fetch(pairs, sems):
    copies = [
        pltpu.make_async_copy(source, target, sems.at[slot])
        for slot, (source, target) in enumerate(pairs)
    ]
    for copy in copies:
        copy.start()
    return copies


def is_even(place_ref):
    return lax.rem(place_ref[0], 2) == 0 if PAIRED else True


def sides_kernel(col_ref, est_ref, obs_ref, even_ref, odd_ref, own_ref, frame_ref, sems):
    for copy in fetch(((est_ref, own_ref), (obs_ref, frame_ref)), sems):
        copy.wait()
    low = low_lanes(TILE)
    first = jnp.where(low, frame_ref[:, 0:LANES], turn(own_ref[:, 0:LANES]))
    last = jnp.where(low, turn(own_ref[:, LANES:TILE]), frame_ref[:, LANES:TILE])
    even = is_even(col_ref)
    even_ref[...] = jnp.where(even, last, first)
    odd_ref[...] = jnp.where(even, first, last)


def ends_kernel(row_ref, col_ref, est_ref, obs_ref, side_even_ref, side_odd_ref, even_ref, odd_ref):
    left, right = ordered(col_ref, side_even_ref, side_odd_ref)
    ends = []
    for est_first, obs_first in ((0, 0), (TILE - MARGIN, TILE - RADIUS)):
        rows = slice(est_first, est_first + MARGIN)
        top = window_rows(est_ref, left(rows), right(rows), rows)
        rows = slice(obs_first, obs_first + RADIUS)
        low = window_rows(obs_ref, turn(left(rows)), turn(right(rows)), rows)
        ends.append((top, low))
    even = is_even(row_ref)
    for part, rows in ((0, slice(0, MARGIN)), (1, slice(MARGIN, HALO))):
        even_ref[rows, :] = jnp.where(even, ends[1][part], ends[0][part])
        odd_ref[rows, :] = jnp.where(even, ends[0][part], ends[1][part])


def ordered(place_ref, even_ref, odd_ref):
    even = is_even(place_ref)
    before = lambda rows: jnp.where(even, odd_ref[rows, :], even_ref[rows, :])
    after = lambda rows: jnp.where(even, even_ref[rows, :], odd_ref[rows, :])
    return before, after


def paired(top, low, near, far):
    a, b, c, d = top[:, near], top[:, far], low[:, near], low[:, far]
    return a - d, b + c, a + d, b - c


def analyse(fold_ref, first, count, col_in_ref, sums_ref):
    for block in range(2):
        cols = slice(block * BLOCK, (block + 1) * BLOCK)
        left = across3(fold_ref, slice(first, first + 2 * count), block * LANES, BLOCK, FRAME)
        put_down(sums_ref, 0, 2 * count, matmul(left, table3(col_in_ref, cols)), cols)


def spectrum(row_ref, sums_ref, count, spec_ref, add):
    for block in range(2):
        near = slice(block * BLOCK, block * BLOCK + LANES)
        far = slice(block * BLOCK + LANES, (block + 1) * BLOCK)
        cols = slice(block * BLOCK, (block + 1) * BLOCK)
        top = matmul(row_ref[0:HALF, :], data3(sums_ref, 0, count, 2 * count, cols))
        low = matmul(row_ref[HALF:FRAME, :], data3(sums_ref, count, count, 2 * count, cols))
        parts = paired(top, low, slice(0, LANES), slice(LANES, BLOCK))
        for part, rows, lanes in zip(
            parts,
            (slice(0, HALF), slice(0, HALF), slice(HALF, FRAME), slice(HALF, FRAME)),
            (near, far, near, far),
            strict=True,
        ):
            spec_ref[rows, lanes] = add[rows, lanes] + part if add is not None else part


def prepare_kernel(
    col_ref, est_ref, obs_ref, side_even_ref, side_odd_ref, bank_ref, table_ref,
    kern_ref, spec_ref, frame_ref,
    raw_ref, wide_ref, tall_ref, fold_ref, sums_ref,
):
    row_own_ref = table_ref.at[0:FRAME, BLOCK : BLOCK + 3 * LANES]
    col_in_ref = table_ref.at[FRAME : FRAME + 2 * BLOCK, 0 : 2 * BLOCK]
    kernel_cols_ref = table_ref.at[FRAME + 2 * BLOCK : FRAME + 3 * BLOCK, 0:BLOCK]
    left, right = ordered(col_ref, side_even_ref, side_odd_ref)
    upper, under = slice(0, LANES), slice(LANES, TILE)
    top = window_rows(est_ref, left(upper), right(upper), upper)
    low = reverse(window_rows(est_ref, left(under), right(under), under))
    put_across(fold_ref, slice(0, LANES), top - low)
    put_across(fold_ref, slice(LANES, TILE), top + low)
    frame_ref[upper, :] = window_rows(obs_ref, turn(left(upper)), turn(right(upper)), upper)
    frame_ref[under, :] = reverse(window_rows(obs_ref, turn(left(under)), turn(right(under)), under))

    shape = (SIDE, SIDE)
    a = lax.broadcasted_iota(jnp.int32, shape, 0).astype(jnp.float32) - RADIUS
    b = lax.broadcasted_iota(jnp.int32, shape, 1).astype(jnp.float32) - RADIUS
    envelope = jnp.exp(-(a * a + b * b) / (2.0 * (0.625 * RADIUS) ** 2))
    raw_ref[...] = jnp.zeros_like(raw_ref)
    for model in range(MODELS):
        raw = bank_ref[:, model, :] * envelope
        total = jnp.sum(jnp.sum(raw, axis=1, keepdims=True), axis=0, keepdims=True)
        raw_ref[model * DEPTH : model * DEPTH + SIDE, 0:SIDE] = raw / total
    put_across(wide_ref, slice(None), raw_ref[...])
    part = matmul(across3(wide_ref, slice(None), 0, LANES, LANES), table3(kernel_cols_ref))
    for model in range(MODELS):
        put_down(tall_ref, 2 * DEPTH * model, DEPTH, part[model * DEPTH : (model + 1) * DEPTH, :])
    gain = 2.0 / (FRAME * BLOCK)
    for model in range(MODELS):
        right = data3(tall_ref, 2 * DEPTH * model, DEPTH, DEPTH)
        top = matmul(table_ref[0:HALF, 0 : 3 * DEPTH], right)
        low = matmul(table_ref[HALF:FRAME, 0 : 3 * DEPTH], right)
        parts = paired(top, low, slice(0, LANES), slice(LANES, BLOCK))
        kern_ref[model, 0:HALF, 0:LANES] = parts[0] * gain
        kern_ref[model, 0:HALF, LANES:BLOCK] = parts[1] * gain
        kern_ref[model, HALF:FRAME, 0:LANES] = parts[2] * gain
        kern_ref[model, HALF:FRAME, LANES:BLOCK] = parts[3] * gain

    analyse(fold_ref, 0, LANES, col_in_ref, sums_ref)
    spectrum(row_own_ref, sums_ref, LANES, spec_ref, None)


def product(spec_ref, kern, block, sign, grown, first, last):
    near = slice(block * BLOCK, block * BLOCK + LANES)
    far = slice(block * BLOCK + LANES, (block + 1) * BLOCK)
    top, low = slice(first, last), slice(HALF + first, HALF + last)
    out = []
    for rows in (top, low):
        fr, fi = spec_ref[rows, near], spec_ref[rows, far]
        kr, ki = kern[rows, 0:LANES], kern[rows, LANES:BLOCK]
        if sign > 0:
            out.append((fr * kr - fi * ki, fr * ki + fi * kr))
        else:
            out.append((fr * kr + fi * ki, fi * kr - fr * ki))
    (ur, ui), (vr, vi) = out
    cos_ref, sin_ref = grown
    put_down(cos_ref, first, HALF, ur + vr, slice(0, LANES))
    put_down(cos_ref, first, HALF, ui + vi, slice(LANES, BLOCK))
    put_down(sin_ref, first, HALF, ui - vi, slice(0, LANES))
    put_down(sin_ref, first, HALF, vr - ur, slice(LANES, BLOCK))


def update_kernel(
    member_ref, row_ref, col_ref, index_ref, cover_ref,
    est_ref, frame_ref, end_even_ref, end_odd_ref, kern_ref, part_ref,
    row_margin_ref, row_in_ref, row_out_ref, col_in_ref, col_out_ref, col_back_ref,
    out_ref,
    fold_ref, sums_ref, spec_ref, cos0_ref, sin0_ref, cos1_ref, sin1_ref, mid0_ref, mid1_ref,
    blur_ref, pick_ref, mask_ref,
):
    member, tile_row, tile_col = member_ref[0], row_ref[0], col_ref[0]
    rows_of_tiles, cols_of_tiles, exposures = cover_ref.shape
    grown = ((cos0_ref, sin0_ref), (cos1_ref, sin1_ref))
    mids = (mid0_ref, mid1_ref)

    above, below = ordered(row_ref, end_even_ref, end_odd_ref)
    top = above(slice(0, MARGIN))
    low = reverse(below(slice(0, MARGIN)))
    put_across(fold_ref, slice(0, MARGIN), top - low)
    put_across(fold_ref, slice(MARGIN, 2 * MARGIN), top + low)
    analyse(fold_ref, 0, MARGIN, col_in_ref, sums_ref)
    spectrum(row_margin_ref, sums_ref, MARGIN, spec_ref, part_ref)

    lane = lax.broadcasted_iota(jnp.int32, (RADIUS, FRAME), 1)
    for step, spans in ((-1, ((LANES, RADIUS),)), (0, ((0, LANES), (FOLD, LANES))), (1, ((FOLD + LANES, RADIUS),))):
        near = []
        for side in (-1, 0, 1):
            r, c = tile_row + step, tile_col + side
            inside = (r >= 0) & (r < rows_of_tiles) & (c >= 0) & (c < cols_of_tiles)
            r = jnp.clip(r, 0, rows_of_tiles - 1)
            c = jnp.clip(c, 0, cols_of_tiles - 1)
            near.append((index_ref[c, r], jnp.where(inside, cover_ref[r, c, member], 0)))

        def spread(which, near=near):
            middle = jnp.where(lane < MARGIN + TILE, near[1][which], near[2][which])
            return jnp.where(lane < MARGIN, near[0][which], middle)

        pick = spread(0)
        cover = jnp.where((lane >= RADIUS) & (lane < FRAME - RADIUS), spread(1), 0)
        for first, count in spans:
            for row in range(first, first + count, RADIUS):
                pick_ref[row : row + RADIUS, :] = pick
                mask_ref[row : row + RADIUS, :] = cover

    def rows_back(block, count, step=None):
        cos_ref, sin_ref = grown[block]
        even = matmul(row_out_ref[0:count, :], data3(cos_ref, 0, HALF, HALF))
        if step is not None:
            step(0)
        odd = matmul(row_out_ref[FOLD : FOLD + count, :], data3(sin_ref, 0, HALF, HALF))
        if step is not None:
            step(1)
        put_across(mids[block], slice(0, count), odd + even)
        put_across(mids[block], slice(count, 2 * count), odd - even)

    def grow(model, block, sign):
        def step(part):
            for first in range(part * HALF // 2, (part + 1) * HALF // 2, 48):
                product(spec_ref, kern_ref.at[model], block, sign, grown[block], first, first + 48)

        return step

    def forward(model, carry):
        rows_back(0, FOLD, grow(model, 1, 1))
        later = jnp.minimum(model + 1, MODELS - 1)
        rows_back(1, FOLD, grow(later, 0, 1))
        one, two = (
            matmul(
                across3(mids[block], slice(0, REACH), 0, BLOCK, BLOCK),
                table3(col_out_ref, slice(block * BLOCK, (block + 1) * BLOCK)),
            )
            for block in range(2)
        )
        for lanes, value in (
            (slice(0, LANES), one[:, 0:LANES]),
            (slice(LANES, BLOCK), one[:, LANES:BLOCK] + two[:, 0:LANES]),
            (slice(BLOCK, FRAME), two[:, LANES:BLOCK]),
        ):
            blur_ref[:, lanes] = jnp.where(pick_ref[:, lanes] == model, value, blur_ref[:, lanes])
        return carry

    grow(0, 0, 1)(0)
    grow(0, 0, 1)(1)
    lax.fori_loop(0, MODELS, forward, 0)

    def ratio(rows, values):
        return jnp.where(mask_ref[rows, :] != 0, values / blur_ref[rows, :], 0.0)

    spare = jnp.zeros((RADIUS, 2 * FRAME), jnp.bfloat16)
    fold_ref[FOLD:HALF, :] = spare
    fold_ref[HALF + FOLD : FRAME, :] = spare
    for row in range(0, LANES, 64):
        top = ratio(slice(row, row + 64), frame_ref[row : row + 64, :])
        low = ratio(slice(FOLD + row, FOLD + row + 64), frame_ref[LANES + row : LANES + row + 64, :])
        put_across(fold_ref, slice(row, row + 64), top - low)
        put_across(fold_ref, slice(HALF + row, HALF + row + 64), top + low)
    top = ratio(slice(LANES, FOLD), above(slice(MARGIN, HALO)))
    low = ratio(slice(FOLD + LANES, REACH), reverse(below(slice(MARGIN, HALO))))
    put_across(fold_ref, slice(LANES, FOLD), top - low)
    put_across(fold_ref, slice(HALF + LANES, HALF + FOLD), top + low)
    analyse(fold_ref, 0, HALF, col_in_ref, sums_ref)
    spectrum(row_in_ref, sums_ref, HALF, spec_ref, None)

    own_model = index_ref[tile_col, tile_row]
    covering = lax.fori_loop(0, exposures, lambda e, n: n + cover_ref[tile_row, tile_col, e], 0)
    own_cover = cover_ref[tile_row, tile_col, member].astype(jnp.float32)
    weight = jnp.full((1, LANES), own_cover, jnp.float32) / jnp.full((1, LANES), covering.astype(jnp.float32), jnp.float32)
    grow(own_model, 0, -1)(0)
    grow(own_model, 0, -1)(1)
    rows_back(0, LANES, grow(own_model, 1, -1))
    rows_back(1, LANES)
    for block in range(2):
        own = slice(block * LANES, (block + 1) * LANES)
        back = matmul(across3(mids[block], slice(0, TILE), 0, BLOCK, BLOCK), table3(col_back_ref, own)) * weight
        out_ref[0:LANES, own] = est_ref[0:LANES, own] * back[0:LANES, :]
        out_ref[LANES:TILE, own] = est_ref[LANES:TILE, own] * reverse(back[LANES:TILE, :])


VMEM = pl.BlockSpec(memory_space=pltpu.VMEM)
SMEM = pl.BlockSpec(memory_space=pltpu.SMEM)


def f32(*shape):
    return jax.ShapeDtypeStruct(shape, jnp.float32)


def half_scratch(*shape):
    return pltpu.VMEM(shape, jnp.bfloat16)


HBM = pl.BlockSpec(memory_space=pltpu.HBM)


def pack_sides(col, estimate, frame):
    return pl.pallas_call(
        sides_kernel,
        out_shape=(f32(TILE, LANES),) * 2 + (f32(TILE, TILE),) * 2,
        in_specs=[SMEM] + [HBM] * 2,
        out_specs=(VMEM,) * 4,
        scratch_shapes=[pltpu.SemaphoreType.DMA((2,))],
        compiler_params=pltpu.CompilerParams(vmem_limit_bytes=4 << 20),
        name="pack_sides",
    )(col, estimate, frame)


def pack_ends(row, col, estimate, frame, side_even, side_odd):
    return pl.pallas_call(
        ends_kernel,
        out_shape=(f32(HALO, FRAME),) * 2,
        in_specs=[SMEM] * 2 + [VMEM] * 4,
        out_specs=(VMEM,) * 2,
        compiler_params=pltpu.CompilerParams(vmem_limit_bytes=4 << 20),
        name="pack_ends",
    )(row, col, estimate, frame, side_even, side_odd)


def prepare(col, estimate, frame, side_even, side_odd, bank, table):
    return pl.pallas_call(
        prepare_kernel,
        out_shape=(f32(MODELS, FRAME, BLOCK), f32(FRAME, 2 * BLOCK), f32(TILE, FRAME)),
        in_specs=[SMEM] + [VMEM] * 6,
        out_specs=(VMEM,) * 3,
        scratch_shapes=[
            pltpu.VMEM((MODELS * DEPTH, LANES), jnp.float32),
            half_scratch(MODELS * DEPTH, 2 * LANES),
            half_scratch(MODELS * 2 * DEPTH, BLOCK),
            half_scratch(TILE, 2 * FRAME),
            half_scratch(2 * TILE, 2 * BLOCK),
        ],
        compiler_params=pltpu.CompilerParams(vmem_limit_bytes=16 << 20),
        cost_estimate=pl.CostEstimate(flops=2 << 30, bytes_accessed=4 << 20, transcendentals=8192),
        name="prepare",
    )(col, estimate, frame, side_even, side_odd, bank, table["ready"])


def tile_update(member, row, col, index, coverage, estimate, frame, end_even, end_odd, spectra, part, table):
    names = ("row_margin", "row_in", "row_out", "col_in", "col_out", "col_back")
    return pl.pallas_call(
        update_kernel,
        out_shape=f32(TILE, TILE),
        in_specs=[SMEM] * 5 + [VMEM] * 12,
        out_specs=VMEM,
        scratch_shapes=[
            half_scratch(FRAME, 2 * FRAME),
            half_scratch(2 * FRAME, 2 * BLOCK),
            pltpu.VMEM((FRAME, 2 * BLOCK), jnp.float32),
            half_scratch(FRAME, BLOCK),
            half_scratch(FRAME, BLOCK),
            half_scratch(FRAME, BLOCK),
            half_scratch(FRAME, BLOCK),
            half_scratch(REACH, 2 * BLOCK),
            half_scratch(REACH, 2 * BLOCK),
            pltpu.VMEM((REACH, FRAME), jnp.float32),
            pltpu.VMEM((REACH, FRAME), jnp.int32),
            pltpu.VMEM((REACH, FRAME), jnp.int32),
        ],
        compiler_params=pltpu.CompilerParams(vmem_limit_bytes=20 << 20),
        cost_estimate=pl.CostEstimate(flops=4 << 30, bytes_accessed=8 << 20, transcendentals=0),
        name="tile_update",
    )(
        member, row, col, index, coverage, estimate, frame, end_even, end_odd, spectra, part,
        *(table[name] for name in names),
    )


def exchange(even, odd, axis):
    count = lax.axis_size(axis)
    if not PAIRED:
        upward = [(i, i + 1) for i in range(count - 1)]
        before = lax.ppermute(even, axis, upward)
        return lax.ppermute(odd, axis, [(b, a) for a, b in upward]), before
    swap = lambda first: [
        step for i in range(first, count - 1, 2) for step in ((i, i + 1), (i + 1, i))
    ]
    outer = lax.ppermute(odd, axis, swap(1))
    return lax.ppermute(even, axis, swap(0)), outer


def exposure_sum(block):
    rows, cols = block.shape
    near = lax.axis_size("exp_y")
    pieces = lax.all_to_all(block.reshape(near, rows // near, cols), "exp_y", 0, 0)
    piece = jnp.sum(pieces, axis=0)
    piece = piece + lax.ppermute(piece, "exp_z", [(0, 1), (1, 0)])
    spread = jnp.broadcast_to(piece[None], (near,) + piece.shape)
    return lax.all_to_all(spread, "exp_y", 0, 0).reshape(rows, cols)


def shards(estimate, observed, psf_bank, psf_index, coverage):
    table = {name: jnp.asarray(value) for name, value in tables().items()}
    frame = observed[0]
    member, row, col = (
        lax.axis_index(axis).astype(jnp.int32).reshape(1)
        for axis in (("exp_y", "exp_z"), "skyx", "skyy")
    )
    bank = psf_bank[0].transpose(1, 0, 2)
    index = psf_index[0].transpose(1, 0)
    cover = coverage.transpose(1, 2, 0)
    *sides, own, frame = pack_sides(col, estimate, frame)
    sides = exchange(*sides, "skyy")
    ends = exchange(*pack_ends(row, col, own, frame, *sides), "skyx")
    spectra, part, folded = prepare(col, own, frame, *sides, bank, table)
    update = tile_update(
        member, row, col, index, cover, own, folded, *ends, spectra, part, table
    )
    return exposure_sum(update)


def solution(mesh):
    exp_count, sky_rows, sky_cols = mesh.devices.shape
    mesh = Mesh(
        mesh.devices.reshape(exp_count // 2, 2, sky_rows, sky_cols),
        ("exp_y", "exp_z", "skyx", "skyy"),
    )
    exp = ("exp_y", "exp_z")
    in_specs = (
        P("skyx", "skyy"),
        P(exp, "skyx", "skyy"),
        P(exp, None, None, None),
        P(exp, None, None),
        P(),
    )
    return jax.shard_map(
        shards, mesh=mesh, in_specs=in_specs, out_specs=P("skyx", "skyy"), check_vma=False
    )
```

```python
import functools

import jax
import jax.numpy as jnp
import numpy as np
from jax import lax
from jax.experimental import pallas as pl
from jax.experimental.pallas import tpu as pltpu
from jax.sharding import Mesh
from jax.sharding import PartitionSpec as P

TILE = 256
RADIUS = 32
SIDE = 2 * RADIUS + 1
MARGIN = 2 * RADIUS
LANES = 128
FRAME = TILE + 2 * MARGIN
HALF = FRAME // 2
BLOCK = 256
HALO = MARGIN + RADIUS
MODELS = 4
REACH = TILE + 2 * RADIUS
FOLD = REACH // 2
DEPTH = 80


def halves(table):
    table = np.asarray(table, np.float32)
    high = table.astype(jnp.bfloat16)
    low = (table - high.astype(np.float32)).astype(jnp.bfloat16)
    return high, low


def waves(places, length):
    frequency = np.arange(length // 2, dtype=np.float64) + 0.5
    angle = 2.0 * np.pi / length * frequency[:, None] * np.asarray(places, np.float64)[None, :]
    return np.concatenate([np.cos(angle), np.sin(angle)], axis=0)


@functools.cache
def tables():
    own = np.arange(MARGIN, HALF) + 0.5
    near = np.arange(RADIUS, MARGIN) + 0.5
    far = np.arange(RADIUS) + 0.5
    margin = np.arange(MARGIN) + 0.5
    starts = (-MARGIN, TILE // 2 - RADIUS)
    column_in = []
    column_out = []
    column_back = []
    for block, start in enumerate(starts):
        column = np.arange(BLOCK) + block * LANES - MARGIN
        place = column - start
        used = (place >= 0) & (place < BLOCK - RADIUS)
        column_in.append((waves(place, BLOCK) * used[None, :]).T)
        first, last = (-RADIUS, LANES) if block == 0 else (LANES, TILE + RADIUS)
        wanted = (column >= first) & (column < last)
        column_out.append(waves(place, BLOCK) * wanted[None, :])
        column_back.append(waves(np.arange(LANES) + block * LANES - start, BLOCK))
    offsets = np.arange(LANES) - RADIUS
    inside = offsets <= RADIUS
    kernel_rows = (waves(offsets, FRAME) * inside[None, :])[:, :DEPTH]
    kernel_cols = (waves(offsets, BLOCK) * inside[None, :]).T

    def across(table):
        high, low = halves(table)
        return np.concatenate([high, high, low], axis=1)

    def pair(table):
        return np.concatenate(halves(table), axis=0)

    def both(places, build=lambda t: t):
        full = waves(places, FRAME)
        return np.concatenate([across(build(full[:HALF])), across(build(full[HALF:]))], axis=0)

    every = np.concatenate([own, near, far])
    ready = np.zeros((FRAME + 3 * BLOCK, BLOCK + 3 * LANES), jnp.bfloat16)
    ready[0:FRAME, 0 : 3 * DEPTH] = across(kernel_rows)
    ready[0:FRAME, BLOCK:] = both(own)
    ready[FRAME : FRAME + 2 * BLOCK, 0 : 2 * BLOCK] = pair(np.concatenate(column_in, axis=1))
    ready[FRAME + 2 * BLOCK :, 0:BLOCK] = pair(kernel_cols)
    return {
        "ready": ready,
        "row_margin": both(margin),
        "row_in": both(every),
        "row_out": both(np.concatenate([own, near]), lambda t: t.T),
        "col_out": pair(np.concatenate(column_out, axis=1)),
        "col_back": pair(np.concatenate(column_back, axis=1)),
    }


def split(value):
    high = value.astype(jnp.bfloat16)
    low = (value - high.astype(jnp.float32)).astype(jnp.bfloat16)
    return high, low


def matmul(left, right):
    return jnp.dot(left, right, preferred_element_type=jnp.float32)


def put_across(ref, rows, value):
    width = value.shape[1]
    ref[rows, 0:width], ref[rows, width : 2 * width] = split(value)


def put_down(ref, row, depth, value, cols=slice(None)):
    count = value.shape[0]
    ref[row : row + count, cols], ref[depth + row : depth + row + count, cols] = split(value)


def across3(ref, rows, first, width, total):
    high = ref[rows, first : first + width]
    return jnp.concatenate([high, ref[rows, total + first : total + first + width], high], axis=1)


def table3(ref, cols=slice(None)):
    depth = ref.shape[0] // 2
    high = ref[0:depth, cols]
    return jnp.concatenate([high, high, ref[depth:, cols]], axis=0)


def data3(ref, first, depth, total, cols=slice(None)):
    high = ref[first : first + depth, cols]
    return jnp.concatenate([high, ref[total + first : total + first + depth, cols], high], axis=0)


def reverse(value):
    count = value.shape[0]
    i = lax.broadcasted_iota(jnp.int32, (count, count), 0)
    j = lax.broadcasted_iota(jnp.int32, (count, count), 1)
    swap = jnp.where(i + j == count - 1, 1.0, 0.0).astype(jnp.bfloat16)
    high, low = split(value)
    return matmul(swap, high) + matmul(swap, low)


def turn(value):
    return pltpu.roll(value, MARGIN, 1)


def low_lanes(rows):
    return lax.broadcasted_iota(jnp.int32, (rows, LANES), 1) < MARGIN


def window_rows(own_ref, left, right, rows):
    low = low_lanes(left.shape[0])
    one, two = turn(own_ref[rows, 0:LANES]), turn(own_ref[rows, LANES:TILE])
    return jnp.concatenate(
        [jnp.where(low, left, one), jnp.where(low, one, two), jnp.where(low, two, right)], axis=1
    )


def is_even(place_ref):
    return lax.rem(place_ref[0], 2) == 0


def ends_kernel(row_ref, est_ref, obs_ref, right_ref, left_ref, even_ref, odd_ref):
    left, right = (lambda rows: left_ref[rows, :]), (lambda rows: right_ref[rows, :])
    ends = []
    for est_first, obs_first in ((0, 0), (TILE - MARGIN, TILE - RADIUS)):
        rows = slice(est_first, est_first + MARGIN)
        top = window_rows(est_ref, left(rows), right(rows), rows)
        rows = slice(obs_first, obs_first + RADIUS)
        low = window_rows(obs_ref, turn(left(rows)), turn(right(rows)), rows)
        ends.append((top, low))
    even = is_even(row_ref)
    for part, rows in ((0, slice(0, MARGIN)), (1, slice(MARGIN, HALO))):
        even_ref[rows, :] = jnp.where(even, ends[1][part], ends[0][part])
        odd_ref[rows, :] = jnp.where(even, ends[0][part], ends[1][part])


def ordered(place_ref, even_ref, odd_ref):
    even = is_even(place_ref)
    before = lambda rows: jnp.where(even, odd_ref[rows, :], even_ref[rows, :])
    after = lambda rows: jnp.where(even, even_ref[rows, :], odd_ref[rows, :])
    return before, after


def paired(top, low, near, far):
    a, b, c, d = top[:, near], top[:, far], low[:, near], low[:, far]
    return a - d, b + c, a + d, b - c


def analyse(fold_ref, first, count, col_in_ref, sums_ref):
    for block in range(2):
        cols = slice(block * BLOCK, (block + 1) * BLOCK)
        left = across3(fold_ref, slice(first, first + 2 * count), block * LANES, BLOCK, FRAME)
        put_down(sums_ref, 0, 2 * count, matmul(left, table3(col_in_ref, cols)), cols)


def spectrum(row_ref, sums_ref, count, spec_ref, add):
    for block in range(2):
        near = slice(block * BLOCK, block * BLOCK + LANES)
        far = slice(block * BLOCK + LANES, (block + 1) * BLOCK)
        cols = slice(block * BLOCK, (block + 1) * BLOCK)
        top = matmul(row_ref[0:HALF, :], data3(sums_ref, 0, count, 2 * count, cols))
        low = matmul(row_ref[HALF:FRAME, :], data3(sums_ref, count, count, 2 * count, cols))
        parts = paired(top, low, slice(0, LANES), slice(LANES, BLOCK))
        for part, rows, lanes in zip(
            parts,
            (slice(0, HALF), slice(0, HALF), slice(HALF, FRAME), slice(HALF, FRAME)),
            (near, far, near, far),
            strict=True,
        ):
            spec_ref[rows, lanes] = add[rows, lanes] + part if add is not None else part


def prepare_kernel(
    est_ref, obs_ref, right_ref, left_ref, bank_ref, table_ref,
    kern_ref, spec_ref, frame_ref,
    raw_ref, wide_ref, tall_ref, fold_ref, sums_ref,
):
    row_own_ref = table_ref.at[0:FRAME, BLOCK : BLOCK + 3 * LANES]
    col_in_ref = table_ref.at[FRAME : FRAME + 2 * BLOCK, 0 : 2 * BLOCK]
    kernel_cols_ref = table_ref.at[FRAME + 2 * BLOCK : FRAME + 3 * BLOCK, 0:BLOCK]
    left, right = (lambda rows: left_ref[rows, :]), (lambda rows: right_ref[rows, :])
    upper, under = slice(0, LANES), slice(LANES, TILE)
    top = window_rows(est_ref, left(upper), right(upper), upper)
    low = reverse(window_rows(est_ref, left(under), right(under), under))
    put_across(fold_ref, slice(0, LANES), top - low)
    put_across(fold_ref, slice(LANES, TILE), top + low)
    frame_ref[upper, :] = window_rows(obs_ref, turn(left(upper)), turn(right(upper)), upper)
    frame_ref[under, :] = reverse(window_rows(obs_ref, turn(left(under)), turn(right(under)), under))

    shape = (SIDE, SIDE)
    a = lax.broadcasted_iota(jnp.int32, shape, 0).astype(jnp.float32) - RADIUS
    b = lax.broadcasted_iota(jnp.int32, shape, 1).astype(jnp.float32) - RADIUS
    envelope = jnp.exp(-(a * a + b * b) / (2.0 * (0.625 * RADIUS) ** 2))
    raw_ref[...] = jnp.zeros_like(raw_ref)
    for model in range(MODELS):
        raw = bank_ref[:, model, :] * envelope
        total = jnp.sum(jnp.sum(raw, axis=1, keepdims=True), axis=0, keepdims=True)
        raw_ref[model * DEPTH : model * DEPTH + SIDE, 0:SIDE] = raw / total
    put_across(wide_ref, slice(None), raw_ref[...])
    part = matmul(across3(wide_ref, slice(None), 0, LANES, LANES), table3(kernel_cols_ref))
    for model in range(MODELS):
        put_down(tall_ref, 2 * DEPTH * model, DEPTH, part[model * DEPTH : (model + 1) * DEPTH, :])
    gain = 2.0 / (FRAME * BLOCK)
    for model in range(MODELS):
        right = data3(tall_ref, 2 * DEPTH * model, DEPTH, DEPTH)
        top = matmul(table_ref[0:HALF, 0 : 3 * DEPTH], right)
        low = matmul(table_ref[HALF:FRAME, 0 : 3 * DEPTH], right)
        parts = paired(top, low, slice(0, LANES), slice(LANES, BLOCK))
        kern_ref[model, 0:HALF, 0:LANES] = parts[0] * gain
        kern_ref[model, 0:HALF, LANES:BLOCK] = parts[1] * gain
        kern_ref[model, HALF:FRAME, 0:LANES] = parts[2] * gain
        kern_ref[model, HALF:FRAME, LANES:BLOCK] = parts[3] * gain

    analyse(fold_ref, 0, LANES, col_in_ref, sums_ref)
    spectrum(row_own_ref, sums_ref, LANES, spec_ref, None)


def product(spec_ref, kern, block, sign, grown, first, last):
    near = slice(block * BLOCK, block * BLOCK + LANES)
    far = slice(block * BLOCK + LANES, (block + 1) * BLOCK)
    top, low = slice(first, last), slice(HALF + first, HALF + last)
    out = []
    for rows in (top, low):
        fr, fi = spec_ref[rows, near], spec_ref[rows, far]
        kr, ki = kern[rows, 0:LANES], kern[rows, LANES:BLOCK]
        if sign > 0:
            out.append((fr * kr - fi * ki, fr * ki + fi * kr))
        else:
            out.append((fr * kr + fi * ki, fi * kr - fr * ki))
    (ur, ui), (vr, vi) = out
    cos_ref, sin_ref = grown
    put_down(cos_ref, first, HALF, ur + vr, slice(0, LANES))
    put_down(cos_ref, first, HALF, ui + vi, slice(LANES, BLOCK))
    put_down(sin_ref, first, HALF, ui - vi, slice(0, LANES))
    put_down(sin_ref, first, HALF, vr - ur, slice(LANES, BLOCK))


def update_kernel(
    member_ref, row_ref, col_ref, index_ref, cover_ref,
    est_ref, frame_ref, end_even_ref, end_odd_ref, kern_ref, part_ref,
    row_margin_ref, row_in_ref, row_out_ref, ready_ref, col_out_ref, col_back_ref,
    out_ref,
    fold_ref, sums_ref, spec_ref, cos0_ref, sin0_ref, cos1_ref, sin1_ref, mid0_ref, mid1_ref,
    blur_ref, pick_ref, mask_ref,
):
    member, tile_row, tile_col = member_ref[0], row_ref[0], col_ref[0]
    rows_of_tiles, cols_of_tiles, exposures = cover_ref.shape
    col_in_ref = ready_ref.at[FRAME : FRAME + 2 * BLOCK, 0 : 2 * BLOCK]
    grown = ((cos0_ref, sin0_ref), (cos1_ref, sin1_ref))
    mids = (mid0_ref, mid1_ref)

    above, below = ordered(row_ref, end_even_ref, end_odd_ref)
    top = above(slice(0, MARGIN))
    low = reverse(below(slice(0, MARGIN)))
    put_across(fold_ref, slice(0, MARGIN), top - low)
    put_across(fold_ref, slice(MARGIN, 2 * MARGIN), top + low)
    analyse(fold_ref, 0, MARGIN, col_in_ref, sums_ref)
    spectrum(row_margin_ref, sums_ref, MARGIN, spec_ref, part_ref)

    lane = lax.broadcasted_iota(jnp.int32, (RADIUS, FRAME), 1)
    for step, spans in ((-1, ((LANES, RADIUS),)), (0, ((0, LANES), (FOLD, LANES))), (1, ((FOLD + LANES, RADIUS),))):
        near = []
        for side in (-1, 0, 1):
            r, c = tile_row + step, tile_col + side
            inside = (r >= 0) & (r < rows_of_tiles) & (c >= 0) & (c < cols_of_tiles)
            r = jnp.clip(r, 0, rows_of_tiles - 1)
            c = jnp.clip(c, 0, cols_of_tiles - 1)
            near.append((index_ref[c, r], jnp.where(inside, cover_ref[r, c, member], 0)))

        def spread(which, near=near):
            middle = jnp.where(lane < MARGIN + TILE, near[1][which], near[2][which])
            return jnp.where(lane < MARGIN, near[0][which], middle)

        pick = spread(0)
        cover = jnp.where((lane >= RADIUS) & (lane < FRAME - RADIUS), spread(1), 0)
        for first, count in spans:
            for row in range(first, first + count, RADIUS):
                pick_ref[row : row + RADIUS, :] = pick
                mask_ref[row : row + RADIUS, :] = cover

    def rows_back(block, count, step=None):
        cos_ref, sin_ref = grown[block]
        even = matmul(row_out_ref[0:count, :], data3(cos_ref, 0, HALF, HALF))
        if step is not None:
            step(0)
        odd = matmul(row_out_ref[FOLD : FOLD + count, :], data3(sin_ref, 0, HALF, HALF))
        if step is not None:
            step(1)
        put_across(mids[block], slice(0, count), odd + even)
        put_across(mids[block], slice(count, 2 * count), odd - even)

    def grow(model, block, sign):
        def step(part):
            for first in range(part * HALF // 2, (part + 1) * HALF // 2, 48):
                product(spec_ref, kern_ref.at[model], block, sign, grown[block], first, first + 48)

        return step

    def forward(model, carry):
        rows_back(0, FOLD, grow(model, 1, 1))
        later = jnp.minimum(model + 1, MODELS - 1)
        rows_back(1, FOLD, grow(later, 0, 1))
        one, two = (
            matmul(
                across3(mids[block], slice(0, REACH), 0, BLOCK, BLOCK),
                table3(col_out_ref, slice(block * BLOCK, (block + 1) * BLOCK)),
            )
            for block in range(2)
        )
        for lanes, value in (
            (slice(0, LANES), one[:, 0:LANES]),
            (slice(LANES, BLOCK), one[:, LANES:BLOCK] + two[:, 0:LANES]),
            (slice(BLOCK, FRAME), two[:, LANES:BLOCK]),
        ):
            blur_ref[:, lanes] = jnp.where(pick_ref[:, lanes] == model, value, blur_ref[:, lanes])
        return carry

    grow(0, 0, 1)(0)
    grow(0, 0, 1)(1)
    lax.fori_loop(0, MODELS, forward, 0)

    def ratio(rows, values):
        return jnp.where(mask_ref[rows, :] != 0, values / blur_ref[rows, :], 0.0)

    spare = jnp.zeros((RADIUS, 2 * FRAME), jnp.bfloat16)
    fold_ref[FOLD:HALF, :] = spare
    fold_ref[HALF + FOLD : FRAME, :] = spare
    for row in range(0, LANES, 64):
        top = ratio(slice(row, row + 64), frame_ref[row : row + 64, :])
        low = ratio(slice(FOLD + row, FOLD + row + 64), frame_ref[LANES + row : LANES + row + 64, :])
        put_across(fold_ref, slice(row, row + 64), top - low)
        put_across(fold_ref, slice(HALF + row, HALF + row + 64), top + low)
    top = ratio(slice(LANES, FOLD), above(slice(MARGIN, HALO)))
    low = ratio(slice(FOLD + LANES, REACH), reverse(below(slice(MARGIN, HALO))))
    put_across(fold_ref, slice(LANES, FOLD), top - low)
    put_across(fold_ref, slice(HALF + LANES, HALF + FOLD), top + low)
    analyse(fold_ref, 0, HALF, col_in_ref, sums_ref)
    spectrum(row_in_ref, sums_ref, HALF, spec_ref, None)

    own_model = index_ref[tile_col, tile_row]
    covering = lax.fori_loop(0, exposures, lambda e, n: n + cover_ref[tile_row, tile_col, e], 0)
    own_cover = cover_ref[tile_row, tile_col, member].astype(jnp.float32)
    weight = jnp.full((1, LANES), own_cover, jnp.float32) / jnp.full((1, LANES), covering.astype(jnp.float32), jnp.float32)
    grow(own_model, 0, -1)(0)
    grow(own_model, 0, -1)(1)
    rows_back(0, LANES, grow(own_model, 1, -1))
    rows_back(1, LANES)
    for block in range(2):
        own = slice(block * LANES, (block + 1) * LANES)
        back = matmul(across3(mids[block], slice(0, TILE), 0, BLOCK, BLOCK), table3(col_back_ref, own)) * weight
        out_ref[0:LANES, own] = est_ref[0:LANES, own] * back[0:LANES, :]
        out_ref[LANES:TILE, own] = est_ref[LANES:TILE, own] * reverse(back[LANES:TILE, :])


VMEM = pl.BlockSpec(memory_space=pltpu.VMEM)
SMEM = pl.BlockSpec(memory_space=pltpu.SMEM)


def f32(*shape):
    return jax.ShapeDtypeStruct(shape, jnp.float32)


def half_scratch(*shape):
    return pltpu.VMEM(shape, jnp.bfloat16)


def pack_ends(row, estimate, frame, side_even, side_odd):
    return pl.pallas_call(
        ends_kernel,
        out_shape=(f32(HALO, FRAME),) * 2,
        in_specs=[SMEM] + [VMEM] * 4,
        out_specs=(VMEM,) * 2,
        compiler_params=pltpu.CompilerParams(vmem_limit_bytes=4 << 20),
        name="pack_ends",
    )(row, estimate, frame, side_even, side_odd)


def prepare(estimate, frame, side_even, side_odd, bank, table):
    return pl.pallas_call(
        prepare_kernel,
        out_shape=(f32(MODELS, FRAME, BLOCK), f32(FRAME, 2 * BLOCK), f32(TILE, FRAME)),
        in_specs=[VMEM] * 6,
        out_specs=(VMEM,) * 3,
        scratch_shapes=[
            pltpu.VMEM((MODELS * DEPTH, LANES), jnp.float32),
            half_scratch(MODELS * DEPTH, 2 * LANES),
            half_scratch(MODELS * 2 * DEPTH, BLOCK),
            half_scratch(TILE, 2 * FRAME),
            half_scratch(2 * TILE, 2 * BLOCK),
        ],
        compiler_params=pltpu.CompilerParams(vmem_limit_bytes=16 << 20),
        cost_estimate=pl.CostEstimate(flops=2 << 30, bytes_accessed=4 << 20, transcendentals=8192),
        name="prepare",
    )(estimate, frame, side_even, side_odd, bank, table["ready"])


def tile_update(member, row, col, index, coverage, estimate, frame, end_even, end_odd, spectra, part, table):
    names = ("row_margin", "row_in", "row_out", "ready", "col_out", "col_back")
    return pl.pallas_call(
        update_kernel,
        out_shape=f32(TILE, TILE),
        in_specs=[SMEM] * 5 + [VMEM] * 12,
        out_specs=VMEM,
        scratch_shapes=[
            half_scratch(FRAME, 2 * FRAME),
            half_scratch(2 * FRAME, 2 * BLOCK),
            pltpu.VMEM((FRAME, 2 * BLOCK), jnp.float32),
            half_scratch(FRAME, BLOCK),
            half_scratch(FRAME, BLOCK),
            half_scratch(FRAME, BLOCK),
            half_scratch(FRAME, BLOCK),
            half_scratch(REACH, 2 * BLOCK),
            half_scratch(REACH, 2 * BLOCK),
            pltpu.VMEM((REACH, FRAME), jnp.float32),
            pltpu.VMEM((REACH, FRAME), jnp.int32),
            pltpu.VMEM((REACH, FRAME), jnp.int32),
        ],
        compiler_params=pltpu.CompilerParams(vmem_limit_bytes=20 << 20),
        cost_estimate=pl.CostEstimate(flops=4 << 30, bytes_accessed=8 << 20, transcendentals=0),
        name="tile_update",
    )(
        member, row, col, index, coverage, estimate, frame, end_even, end_odd, spectra, part,
        *(table[name] for name in names),
    )


def exchange(even, odd, axis):
    count = lax.axis_size(axis)
    swap = lambda first: [
        step for i in range(first, count - 1, 2) for step in ((i, i + 1), (i + 1, i))
    ]
    near = lax.ppermute(even, axis, swap(0))
    return near, lax.ppermute(odd, axis, swap(1))


def exposure_sum(block):
    rows, cols = block.shape
    near = lax.axis_size("exp_y")
    pieces = lax.all_to_all(block.reshape(near, rows // near, cols), "exp_y", 0, 0)
    piece = jnp.sum(pieces, axis=0)
    piece = piece + lax.ppermute(piece, "exp_z", [(0, 1), (1, 0)])
    spread = jnp.broadcast_to(piece[None], (near,) + piece.shape)
    return lax.all_to_all(spread, "exp_y", 0, 0).reshape(rows, cols)


def shards(estimate, observed, psf_bank, psf_index, coverage):
    table = {name: jnp.asarray(value) for name, value in tables().items()}
    frame = observed[0]
    member, row, col = (
        lax.axis_index(axis).astype(jnp.int32).reshape(1)
        for axis in (("exp_y", "exp_z"), "skyx", "skyy")
    )
    bank = psf_bank[0].transpose(1, 0, 2)
    index = psf_index[0].transpose(1, 0)
    cover = coverage.transpose(1, 2, 0)
    own = estimate
    first = jnp.concatenate([frame[:, :MARGIN], own[:, :MARGIN]], axis=1)
    last = jnp.concatenate([own[:, TILE - MARGIN :], frame[:, TILE - MARGIN :]], axis=1)
    upward = [(i, i + 1) for i in range(lax.axis_size("skyy") - 1)]
    sides = (
        lax.ppermute(first, "skyy", [(b, a) for a, b in upward]),
        lax.ppermute(last, "skyy", upward),
    )
    ends = exchange(*pack_ends(row, own, frame, *sides), "skyx")
    spectra, part, folded = prepare(own, frame, *sides, bank, table)
    update = tile_update(
        member, row, col, index, cover, own, folded, *ends, spectra, part, table
    )
    return exposure_sum(update)


def solution(mesh):
    exp_count, sky_rows, sky_cols = mesh.devices.shape
    mesh = Mesh(
        mesh.devices.reshape(exp_count // 2, 2, sky_rows, sky_cols),
        ("exp_y", "exp_z", "skyx", "skyy"),
    )
    exp = ("exp_y", "exp_z")
    in_specs = (
        P("skyx", "skyy"),
        P(exp, "skyx", "skyy"),
        P(exp, None, None, None),
        P(exp, None, None),
        P(),
    )
    return jax.shard_map(
        shards, mesh=mesh, in_specs=in_specs, out_specs=P("skyx", "skyy"), check_vma=False
    )
```

```python
import functools

import jax
import jax.numpy as jnp
import numpy as np
from jax import lax
from jax.experimental import pallas as pl
from jax.experimental.pallas import tpu as pltpu
from jax.sharding import Mesh
from jax.sharding import PartitionSpec as P

TILE = 256
RADIUS = 32
SIDE = 2 * RADIUS + 1
MARGIN = 2 * RADIUS
LANES = 128
FRAME = TILE + 2 * MARGIN
HALF = FRAME // 2
BLOCK = 256
HALO = MARGIN + RADIUS
MODELS = 4
REACH = TILE + 2 * RADIUS
FOLD = REACH // 2
DEPTH = 80


def halves(table):
    table = np.asarray(table, np.float32)
    high = table.astype(jnp.bfloat16)
    low = (table - high.astype(np.float32)).astype(jnp.bfloat16)
    return high, low


def waves(places, length):
    frequency = np.arange(length // 2, dtype=np.float64) + 0.5
    angle = 2.0 * np.pi / length * frequency[:, None] * np.asarray(places, np.float64)[None, :]
    return np.concatenate([np.cos(angle), np.sin(angle)], axis=0)


@functools.cache
def tables():
    own = np.arange(MARGIN, HALF) + 0.5
    near = np.arange(RADIUS, MARGIN) + 0.5
    far = np.arange(RADIUS) + 0.5
    margin = np.arange(MARGIN) + 0.5
    starts = (-MARGIN, TILE // 2 - RADIUS)
    column_in = []
    column_out = []
    column_back = []
    for block, start in enumerate(starts):
        column = np.arange(BLOCK) + block * LANES - MARGIN
        place = column - start
        used = (place >= 0) & (place < BLOCK - RADIUS)
        column_in.append((waves(place, BLOCK) * used[None, :]).T)
        first, last = (-RADIUS, LANES) if block == 0 else (LANES, TILE + RADIUS)
        wanted = (column >= first) & (column < last)
        column_out.append(waves(place, BLOCK) * wanted[None, :])
        column_back.append(waves(np.arange(LANES) + block * LANES - start, BLOCK))
    offsets = np.arange(LANES) - RADIUS
    inside = offsets <= RADIUS
    kernel_rows = (waves(offsets, FRAME) * inside[None, :])[:, :DEPTH]
    kernel_cols = (waves(offsets, BLOCK) * inside[None, :]).T

    def across(table):
        high, low = halves(table)
        return np.concatenate([high, high, low], axis=1)

    def pair(table):
        return np.concatenate(halves(table), axis=0)

    def both(places, build=lambda t: t):
        full = waves(places, FRAME)
        return np.concatenate([across(build(full[:HALF])), across(build(full[HALF:]))], axis=0)

    every = np.concatenate([own, near, far])
    ready = np.zeros((FRAME + 3 * BLOCK, BLOCK + 3 * LANES), jnp.bfloat16)
    ready[0:FRAME, 0 : 3 * DEPTH] = across(kernel_rows)
    ready[0:FRAME, BLOCK:] = both(own)
    ready[FRAME : FRAME + 2 * BLOCK, 0 : 2 * BLOCK] = pair(np.concatenate(column_in, axis=1))
    ready[FRAME + 2 * BLOCK :, 0:BLOCK] = pair(kernel_cols)
    return {
        "ready": ready,
        "row_margin": both(margin),
        "row_in": both(every),
        "row_out": both(np.concatenate([own, near]), lambda t: t.T),
        "col_out": pair(np.concatenate(column_out, axis=1)),
        "col_back": pair(np.concatenate(column_back, axis=1)),
    }


def split(value):
    high = value.astype(jnp.bfloat16)
    low = (value - high.astype(jnp.float32)).astype(jnp.bfloat16)
    return high, low


def matmul(left, right):
    return jnp.dot(left, right, preferred_element_type=jnp.float32)


def put_across(ref, rows, value):
    width = value.shape[1]
    ref[rows, 0:width], ref[rows, width : 2 * width] = split(value)


def put_down(ref, row, depth, value, cols=slice(None)):
    count = value.shape[0]
    ref[row : row + count, cols], ref[depth + row : depth + row + count, cols] = split(value)


def across3(ref, rows, first, width, total):
    high = ref[rows, first : first + width]
    return jnp.concatenate([high, ref[rows, total + first : total + first + width], high], axis=1)


def table3(ref, cols=slice(None)):
    depth = ref.shape[0] // 2
    high = ref[0:depth, cols]
    return jnp.concatenate([high, high, ref[depth:, cols]], axis=0)


def data3(ref, first, depth, total, cols=slice(None)):
    high = ref[first : first + depth, cols]
    return jnp.concatenate([high, ref[total + first : total + first + depth, cols], high], axis=0)


def reverse(value):
    count = value.shape[0]
    i = lax.broadcasted_iota(jnp.int32, (count, count), 0)
    j = lax.broadcasted_iota(jnp.int32, (count, count), 1)
    swap = jnp.where(i + j == count - 1, 1.0, 0.0).astype(jnp.bfloat16)
    high, low = split(value)
    return matmul(swap, high) + matmul(swap, low)


def turn(value):
    return pltpu.roll(value, MARGIN, 1)


def low_lanes(rows):
    return lax.broadcasted_iota(jnp.int32, (rows, LANES), 1) < MARGIN


def window_rows(own_ref, left, right, rows):
    low = low_lanes(left.shape[0])
    one, two = turn(own_ref[rows, 0:LANES]), turn(own_ref[rows, LANES:TILE])
    return jnp.concatenate(
        [jnp.where(low, left, one), jnp.where(low, one, two), jnp.where(low, two, right)], axis=1
    )


def ends_kernel(row_ref, est_ref, obs_ref, left_ref, right_ref, pair_ref, outer_ref):
    even = lax.rem(row_ref[0], 2) == 0
    ends = []
    for est_first, obs_first in ((0, 0), (TILE - MARGIN, TILE - RADIUS)):
        rows = slice(est_first, est_first + MARGIN)
        top = window_rows(est_ref, left_ref[rows, :], right_ref[rows, :], rows)
        rows = slice(obs_first, obs_first + RADIUS)
        low = window_rows(obs_ref, turn(left_ref[rows, :]), turn(right_ref[rows, :]), rows)
        ends.append((top, low))
    for part, rows in ((0, slice(0, MARGIN)), (1, slice(MARGIN, HALO))):
        pair_ref[rows, :] = jnp.where(even, ends[1][part], ends[0][part])
        outer_ref[rows, :] = jnp.where(even, ends[0][part], ends[1][part])


def paired(top, low, near, far):
    a, b, c, d = top[:, near], top[:, far], low[:, near], low[:, far]
    return a - d, b + c, a + d, b - c


def analyse(fold_ref, first, count, col_in_ref, sums_ref):
    for block in range(2):
        cols = slice(block * BLOCK, (block + 1) * BLOCK)
        left = across3(fold_ref, slice(first, first + 2 * count), block * LANES, BLOCK, FRAME)
        put_down(sums_ref, 0, 2 * count, matmul(left, table3(col_in_ref, cols)), cols)


def spectrum(row_ref, sums_ref, count, spec_ref, add):
    for block in range(2):
        near = slice(block * BLOCK, block * BLOCK + LANES)
        far = slice(block * BLOCK + LANES, (block + 1) * BLOCK)
        cols = slice(block * BLOCK, (block + 1) * BLOCK)
        top = matmul(row_ref[0:HALF, :], data3(sums_ref, 0, count, 2 * count, cols))
        low = matmul(row_ref[HALF:FRAME, :], data3(sums_ref, count, count, 2 * count, cols))
        parts = paired(top, low, slice(0, LANES), slice(LANES, BLOCK))
        for part, rows, lanes in zip(
            parts,
            (slice(0, HALF), slice(0, HALF), slice(HALF, FRAME), slice(HALF, FRAME)),
            (near, far, near, far),
            strict=True,
        ):
            spec_ref[rows, lanes] = add[rows, lanes] + part if add is not None else part


def prepare_kernel(
    est_ref, obs_ref, left_ref, right_ref, bank_ref, table_ref,
    kern_ref, spec_ref, frame_ref,
    raw_ref, wide_ref, tall_ref, fold_ref, sums_ref,
):
    row_own_ref = table_ref.at[0:FRAME, BLOCK : BLOCK + 3 * LANES]
    col_in_ref = table_ref.at[FRAME : FRAME + 2 * BLOCK, 0 : 2 * BLOCK]
    kernel_cols_ref = table_ref.at[FRAME + 2 * BLOCK : FRAME + 3 * BLOCK, 0:BLOCK]
    left, right = (lambda rows: left_ref[rows, :]), (lambda rows: right_ref[rows, :])
    upper, under = slice(0, LANES), slice(LANES, TILE)
    top = window_rows(est_ref, left(upper), right(upper), upper)
    low = reverse(window_rows(est_ref, left(under), right(under), under))
    put_across(fold_ref, slice(0, LANES), top - low)
    put_across(fold_ref, slice(LANES, TILE), top + low)
    frame_ref[upper, :] = window_rows(obs_ref, turn(left(upper)), turn(right(upper)), upper)
    frame_ref[under, :] = reverse(window_rows(obs_ref, turn(left(under)), turn(right(under)), under))

    shape = (SIDE, SIDE)
    a = lax.broadcasted_iota(jnp.int32, shape, 0).astype(jnp.float32) - RADIUS
    b = lax.broadcasted_iota(jnp.int32, shape, 1).astype(jnp.float32) - RADIUS
    envelope = jnp.exp(-(a * a + b * b) / (2.0 * (0.625 * RADIUS) ** 2))
    raw_ref[...] = jnp.zeros_like(raw_ref)
    for model in range(MODELS):
        raw = bank_ref[:, model, :] * envelope
        total = jnp.sum(jnp.sum(raw, axis=1, keepdims=True), axis=0, keepdims=True)
        raw_ref[model * DEPTH : model * DEPTH + SIDE, 0:SIDE] = raw / total
    put_across(wide_ref, slice(None), raw_ref[...])
    part = matmul(across3(wide_ref, slice(None), 0, LANES, LANES), table3(kernel_cols_ref))
    for model in range(MODELS):
        put_down(tall_ref, 2 * DEPTH * model, DEPTH, part[model * DEPTH : (model + 1) * DEPTH, :])
    gain = 2.0 / (FRAME * BLOCK)
    for model in range(MODELS):
        right = data3(tall_ref, 2 * DEPTH * model, DEPTH, DEPTH)
        top = matmul(table_ref[0:HALF, 0 : 3 * DEPTH], right)
        low = matmul(table_ref[HALF:FRAME, 0 : 3 * DEPTH], right)
        parts = paired(top, low, slice(0, LANES), slice(LANES, BLOCK))
        kern_ref[model, 0:HALF, 0:LANES] = parts[0] * gain
        kern_ref[model, 0:HALF, LANES:BLOCK] = parts[1] * gain
        kern_ref[model, HALF:FRAME, 0:LANES] = parts[2] * gain
        kern_ref[model, HALF:FRAME, LANES:BLOCK] = parts[3] * gain

    analyse(fold_ref, 0, LANES, col_in_ref, sums_ref)
    spectrum(row_own_ref, sums_ref, LANES, spec_ref, None)


def product(spec_ref, kern, block, sign, grown, first, last):
    near = slice(block * BLOCK, block * BLOCK + LANES)
    far = slice(block * BLOCK + LANES, (block + 1) * BLOCK)
    top, low = slice(first, last), slice(HALF + first, HALF + last)
    out = []
    for rows in (top, low):
        fr, fi = spec_ref[rows, near], spec_ref[rows, far]
        kr, ki = kern[rows, 0:LANES], kern[rows, LANES:BLOCK]
        if sign > 0:
            out.append((fr * kr - fi * ki, fr * ki + fi * kr))
        else:
            out.append((fr * kr + fi * ki, fi * kr - fr * ki))
    (ur, ui), (vr, vi) = out
    cos_ref, sin_ref = grown
    put_down(cos_ref, first, HALF, ur + vr, slice(0, LANES))
    put_down(cos_ref, first, HALF, ui + vi, slice(LANES, BLOCK))
    put_down(sin_ref, first, HALF, ui - vi, slice(0, LANES))
    put_down(sin_ref, first, HALF, vr - ur, slice(LANES, BLOCK))


def maps_kernel(
    member_ref, row_ref, col_ref, index_ref, cover_ref, pick_ref, mask_ref, own_ref, odd_ref, weight_ref
):
    member, tile_row, tile_col = member_ref[0], row_ref[0], col_ref[0]
    rows_of_tiles, cols_of_tiles, exposures = cover_ref.shape
    lane = lax.broadcasted_iota(jnp.int32, (RADIUS, FRAME), 1)
    for step, spans in ((-1, ((LANES, RADIUS),)), (0, ((0, LANES), (FOLD, LANES))), (1, ((FOLD + LANES, RADIUS),))):
        near = []
        for side in (-1, 0, 1):
            r, c = tile_row + step, tile_col + side
            inside = (r >= 0) & (r < rows_of_tiles) & (c >= 0) & (c < cols_of_tiles)
            r = jnp.clip(r, 0, rows_of_tiles - 1)
            c = jnp.clip(c, 0, cols_of_tiles - 1)
            near.append((index_ref[c, r], jnp.where(inside, cover_ref[r, c, member], 0)))

        def spread(which, near=near):
            middle = jnp.where(lane < MARGIN + TILE, near[1][which], near[2][which])
            return jnp.where(lane < MARGIN, near[0][which], middle)

        pick = spread(0)
        cover = jnp.where((lane >= RADIUS) & (lane < FRAME - RADIUS), spread(1), 0)
        for first, count in spans:
            for row in range(first, first + count, RADIUS):
                pick_ref[row : row + RADIUS, :] = pick
                mask_ref[row : row + RADIUS, :] = cover

    covering = lax.fori_loop(0, exposures, lambda e, n: n + cover_ref[tile_row, tile_col, e], 0)
    own_cover = cover_ref[tile_row, tile_col, member].astype(jnp.float32)
    own_ref[...] = jnp.full(own_ref.shape, index_ref[tile_col, tile_row], jnp.int32)
    odd_ref[...] = jnp.full(odd_ref.shape, lax.rem(tile_row, 2), jnp.int32)
    weight_ref[...] = jnp.full(weight_ref.shape, own_cover, jnp.float32) / jnp.full(
        weight_ref.shape, covering.astype(jnp.float32), jnp.float32
    )


def update_kernel(
    pick_ref, mask_ref, own_ref, odd_ref, weight_ref,
    est_ref, frame_ref, pair_ref, outer_ref, kern_ref, part_ref,
    row_margin_ref, row_in_ref, row_out_ref, ready_ref, col_out_ref, col_back_ref,
    out_ref,
    fold_ref, sums_ref, spec_ref, cos0_ref, sin0_ref, cos1_ref, sin1_ref, mid0_ref, mid1_ref,
    blur_ref, own_kern_ref,
):
    col_in_ref = ready_ref.at[FRAME : FRAME + 2 * BLOCK, 0 : 2 * BLOCK]
    grown = ((cos0_ref, sin0_ref), (cos1_ref, sin1_ref))
    mids = (mid0_ref, mid1_ref)

    odd = odd_ref[0:1, :] != 0
    above = jnp.where(odd, pair_ref[...], outer_ref[...])
    below = jnp.where(odd, outer_ref[...], pair_ref[...])
    top = above[0:MARGIN, :]
    low = reverse(below[0:MARGIN, :])
    put_across(fold_ref, slice(0, MARGIN), top - low)
    put_across(fold_ref, slice(MARGIN, 2 * MARGIN), top + low)
    analyse(fold_ref, 0, MARGIN, col_in_ref, sums_ref)
    spectrum(row_margin_ref, sums_ref, MARGIN, spec_ref, part_ref)

    own = own_ref[0:1, :]
    for row in range(0, FRAME, 48):
        rows = slice(row, row + 48)
        for lanes in (slice(0, LANES), slice(LANES, BLOCK)):
            chosen = kern_ref[0, rows, lanes]
            for model in range(1, MODELS):
                chosen = jnp.where(own == model, kern_ref[model, rows, lanes], chosen)
            own_kern_ref[rows, lanes] = chosen

    def rows_back(block, count, step=None):
        cos_ref, sin_ref = grown[block]
        even = matmul(row_out_ref[0:count, :], data3(cos_ref, 0, HALF, HALF))
        if step is not None:
            step(0)
        odd = matmul(row_out_ref[FOLD : FOLD + count, :], data3(sin_ref, 0, HALF, HALF))
        if step is not None:
            step(1)
        put_across(mids[block], slice(0, count), odd + even)
        put_across(mids[block], slice(count, 2 * count), odd - even)

    def grow(kern, block, sign):
        def step(part):
            for first in range(part * HALF // 2, (part + 1) * HALF // 2, 48):
                product(spec_ref, kern, block, sign, grown[block], first, first + 48)

        return step

    def forward(model, carry):
        rows_back(0, FOLD, grow(kern_ref.at[model], 1, 1))
        later = jnp.minimum(model + 1, MODELS - 1)
        rows_back(1, FOLD, grow(kern_ref.at[later], 0, 1))
        one, two = (
            matmul(
                across3(mids[block], slice(0, REACH), 0, BLOCK, BLOCK),
                table3(col_out_ref, slice(block * BLOCK, (block + 1) * BLOCK)),
            )
            for block in range(2)
        )
        for lanes, value in (
            (slice(0, LANES), one[:, 0:LANES]),
            (slice(LANES, BLOCK), one[:, LANES:BLOCK] + two[:, 0:LANES]),
            (slice(BLOCK, FRAME), two[:, LANES:BLOCK]),
        ):
            blur_ref[:, lanes] = jnp.where(pick_ref[:, lanes] == model, value, blur_ref[:, lanes])
        return carry

    grow(kern_ref.at[0], 0, 1)(0)
    grow(kern_ref.at[0], 0, 1)(1)
    lax.fori_loop(0, MODELS, forward, 0)

    def ratio(rows, values):
        return jnp.where(mask_ref[rows, :] != 0, values / blur_ref[rows, :], 0.0)

    spare = jnp.zeros((RADIUS, 2 * FRAME), jnp.bfloat16)
    fold_ref[FOLD:HALF, :] = spare
    fold_ref[HALF + FOLD : FRAME, :] = spare
    for row in range(0, LANES, 64):
        top = ratio(slice(row, row + 64), frame_ref[row : row + 64, :])
        low = ratio(slice(FOLD + row, FOLD + row + 64), frame_ref[LANES + row : LANES + row + 64, :])
        put_across(fold_ref, slice(row, row + 64), top - low)
        put_across(fold_ref, slice(HALF + row, HALF + row + 64), top + low)
    top = ratio(slice(LANES, FOLD), above[MARGIN:HALO, :])
    low = ratio(slice(FOLD + LANES, REACH), reverse(below[MARGIN:HALO, :]))
    put_across(fold_ref, slice(LANES, FOLD), top - low)
    put_across(fold_ref, slice(HALF + LANES, HALF + FOLD), top + low)
    analyse(fold_ref, 0, HALF, col_in_ref, sums_ref)
    spectrum(row_in_ref, sums_ref, HALF, spec_ref, None)

    weight = weight_ref[0:1, :]
    grow(own_kern_ref, 0, -1)(0)
    grow(own_kern_ref, 0, -1)(1)
    rows_back(0, LANES, grow(own_kern_ref, 1, -1))
    rows_back(1, LANES)
    for block in range(2):
        own = slice(block * LANES, (block + 1) * LANES)
        back = matmul(across3(mids[block], slice(0, TILE), 0, BLOCK, BLOCK), table3(col_back_ref, own)) * weight
        out_ref[0:LANES, own] = est_ref[0:LANES, own] * back[0:LANES, :]
        out_ref[LANES:TILE, own] = est_ref[LANES:TILE, own] * reverse(back[LANES:TILE, :])


VMEM = pl.BlockSpec(memory_space=pltpu.VMEM)
SMEM = pl.BlockSpec(memory_space=pltpu.SMEM)


def f32(*shape):
    return jax.ShapeDtypeStruct(shape, jnp.float32)


def half_scratch(*shape):
    return pltpu.VMEM(shape, jnp.bfloat16)


def pack_ends(row, estimate, frame, left, right):
    return pl.pallas_call(
        ends_kernel,
        out_shape=(f32(HALO, FRAME),) * 2,
        in_specs=[SMEM] + [VMEM] * 4,
        out_specs=(VMEM,) * 2,
        compiler_params=pltpu.CompilerParams(vmem_limit_bytes=4 << 20),
        name="pack_ends",
    )(row, estimate, frame, left, right)


def pixel_maps(member, row, col, index, coverage):
    whole = jax.ShapeDtypeStruct((REACH, FRAME), jnp.int32)
    small = (8, LANES)
    return pl.pallas_call(
        maps_kernel,
        out_shape=(
            whole, whole, jax.ShapeDtypeStruct(small, jnp.int32),
            jax.ShapeDtypeStruct((8, FRAME), jnp.int32), f32(*small),
        ),
        in_specs=[SMEM] * 5,
        out_specs=(VMEM,) * 5,
        compiler_params=pltpu.CompilerParams(vmem_limit_bytes=4 << 20),
        cost_estimate=pl.CostEstimate(flops=1 << 28, bytes_accessed=1 << 20, transcendentals=0),
        name="pixel_maps",
    )(member, row, col, index, coverage)


def prepare(estimate, frame, left, right, bank, table):
    return pl.pallas_call(
        prepare_kernel,
        out_shape=(f32(MODELS, FRAME, BLOCK), f32(FRAME, 2 * BLOCK), f32(TILE, FRAME)),
        in_specs=[VMEM] * 6,
        out_specs=(VMEM,) * 3,
        scratch_shapes=[
            pltpu.VMEM((MODELS * DEPTH, LANES), jnp.float32),
            half_scratch(MODELS * DEPTH, 2 * LANES),
            half_scratch(MODELS * 2 * DEPTH, BLOCK),
            half_scratch(TILE, 2 * FRAME),
            half_scratch(2 * TILE, 2 * BLOCK),
        ],
        compiler_params=pltpu.CompilerParams(vmem_limit_bytes=16 << 20),
        cost_estimate=pl.CostEstimate(flops=2 << 30, bytes_accessed=4 << 20, transcendentals=8192),
        name="prepare",
    )(estimate, frame, left, right, bank, table["ready"])


def tile_update(maps, estimate, frame, pair, outer, spectra, part, table):
    names = ("row_margin", "row_in", "row_out", "ready", "col_out", "col_back")
    return pl.pallas_call(
        update_kernel,
        out_shape=f32(TILE, TILE),
        in_specs=[VMEM] * 17,
        out_specs=VMEM,
        scratch_shapes=[
            half_scratch(FRAME, 2 * FRAME),
            half_scratch(2 * FRAME, 2 * BLOCK),
            pltpu.VMEM((FRAME, 2 * BLOCK), jnp.float32),
            half_scratch(FRAME, BLOCK),
            half_scratch(FRAME, BLOCK),
            half_scratch(FRAME, BLOCK),
            half_scratch(FRAME, BLOCK),
            half_scratch(REACH, 2 * BLOCK),
            half_scratch(REACH, 2 * BLOCK),
            pltpu.VMEM((REACH, FRAME), jnp.float32),
            pltpu.VMEM((FRAME, BLOCK), jnp.float32),
        ],
        compiler_params=pltpu.CompilerParams(vmem_limit_bytes=20 << 20),
        cost_estimate=pl.CostEstimate(flops=4 << 30, bytes_accessed=8 << 20, transcendentals=0),
        name="tile_update",
    )(
        *maps, estimate, frame, pair, outer, spectra, part,
        *(table[name] for name in names),
    )


def exchange(first, last, axis):
    upward = [(i, i + 1) for i in range(lax.axis_size(axis) - 1)]
    after = lax.ppermute(first, axis, [(b, a) for a, b in upward])
    return lax.ppermute(last, axis, upward), after


def trade(pair, outer, axis):
    count = lax.axis_size(axis)
    swap = lambda first: [
        step for i in range(first, count - 1, 2) for step in ((i, i + 1), (i + 1, i))
    ]
    return lax.ppermute(pair, axis, swap(0)), lax.ppermute(outer, axis, swap(1))


def exposure_sum(block):
    rows, cols = block.shape
    near = lax.axis_size("exp_y")
    pieces = lax.all_to_all(block.reshape(near, rows // near, cols), "exp_y", 0, 0)
    piece = jnp.sum(pieces, axis=0)
    piece = piece + lax.ppermute(piece, "exp_z", [(0, 1), (1, 0)])
    spread = jnp.broadcast_to(piece[None], (near,) + piece.shape)
    return lax.all_to_all(spread, "exp_y", 0, 0).reshape(rows, cols)


def shards(estimate, observed, psf_bank, psf_index, coverage):
    table = {name: jnp.asarray(value) for name, value in tables().items()}
    frame = observed[0]
    member, row, col = (
        lax.axis_index(axis).astype(jnp.int32).reshape(1)
        for axis in (("exp_y", "exp_z"), "skyx", "skyy")
    )
    bank = psf_bank[0].transpose(1, 0, 2)
    index = psf_index[0].transpose(1, 0)
    cover = coverage.transpose(1, 2, 0)
    own = estimate
    first = jnp.concatenate([frame[:, :MARGIN], own[:, :MARGIN]], axis=1)
    last = jnp.concatenate([own[:, TILE - MARGIN :], frame[:, TILE - MARGIN :]], axis=1)
    sides = exchange(first, last, "skyy")
    maps = pixel_maps(member, row, col, index, cover)
    ends = trade(*pack_ends(row, own, frame, *sides), "skyx")
    spectra, part, folded = prepare(own, frame, *sides, bank, table)
    update = tile_update(maps, own, folded, *ends, spectra, part, table)
    return exposure_sum(update)


def solution(mesh):
    exp_count, sky_rows, sky_cols = mesh.devices.shape
    mesh = Mesh(
        mesh.devices.reshape(exp_count // 2, 2, sky_rows, sky_cols),
        ("exp_y", "exp_z", "skyx", "skyy"),
    )
    exp = ("exp_y", "exp_z")
    in_specs = (
        P("skyx", "skyy"),
        P(exp, "skyx", "skyy"),
        P(exp, None, None, None),
        P(exp, None, None),
        P(),
    )
    return jax.shard_map(
        shards, mesh=mesh, in_specs=in_specs, out_specs=P("skyx", "skyy"), check_vma=False
    )
```

```python
import functools

import jax
import jax.numpy as jnp
import numpy as np
from jax import lax
from jax.experimental import pallas as pl
from jax.experimental.pallas import tpu as pltpu
from jax.sharding import Mesh
from jax.sharding import PartitionSpec as P

TILE = 256
RADIUS = 32
SIDE = 2 * RADIUS + 1
MARGIN = 2 * RADIUS
LANES = 128
FRAME = TILE + 2 * MARGIN
HALF = FRAME // 2
BLOCK = 256
HALO = MARGIN + RADIUS
MODELS = 4
REACH = TILE + 2 * RADIUS
FOLD = REACH // 2
DEPTH = 80


def halves(table):
    table = np.asarray(table, np.float32)
    high = table.astype(jnp.bfloat16)
    low = (table - high.astype(np.float32)).astype(jnp.bfloat16)
    return high, low


def waves(places, length):
    frequency = np.arange(length // 2, dtype=np.float64) + 0.5
    angle = 2.0 * np.pi / length * frequency[:, None] * np.asarray(places, np.float64)[None, :]
    return np.concatenate([np.cos(angle), np.sin(angle)], axis=0)


@functools.cache
def tables():
    own = np.arange(MARGIN, HALF) + 0.5
    near = np.arange(RADIUS, MARGIN) + 0.5
    far = np.arange(RADIUS) + 0.5
    margin = np.arange(MARGIN) + 0.5
    starts = (-MARGIN, TILE // 2 - RADIUS)
    column_in = []
    column_out = []
    for block, start in enumerate(starts):
        column = np.arange(BLOCK) + block * LANES - MARGIN
        place = column - start
        used = (place >= 0) & (place < BLOCK - RADIUS)
        column_in.append((waves(place, BLOCK) * used[None, :]).T)
        first, last = (-RADIUS, LANES) if block == 0 else (LANES, TILE + RADIUS)
        wanted = (column >= first) & (column < last)
        column_out.append(waves(place, BLOCK) * wanted[None, :])
    offsets = np.arange(LANES) - RADIUS
    inside = offsets <= RADIUS
    kernel_rows = (waves(offsets, FRAME) * inside[None, :])[:, :DEPTH]
    kernel_cols = (waves(offsets, BLOCK) * inside[None, :]).T

    def across(table):
        high, low = halves(table)
        return np.concatenate([high, high, low], axis=1)

    def pair(table):
        return np.concatenate(halves(table), axis=0)

    def both(places, build=lambda t: t):
        full = waves(places, FRAME)
        return np.concatenate([across(build(full[:HALF])), across(build(full[HALF:]))], axis=0)

    every = np.concatenate([own, near, far])
    ready = np.zeros((FRAME + 3 * BLOCK, BLOCK + 3 * LANES), jnp.bfloat16)
    ready[0:FRAME, 0 : 3 * DEPTH] = across(kernel_rows)
    ready[0:FRAME, BLOCK:] = both(own)
    ready[FRAME : FRAME + 2 * BLOCK, 0 : 2 * BLOCK] = pair(np.concatenate(column_in, axis=1))
    ready[FRAME + 2 * BLOCK :, 0:BLOCK] = pair(kernel_cols)
    return {
        "ready": ready,
        "row_margin": both(margin),
        "row_in": both(every),
        "row_out": both(np.concatenate([own, near]), lambda t: t.T),
        "col_out": pair(np.concatenate(column_out, axis=1)),
    }


def split(value):
    high = value.astype(jnp.bfloat16)
    low = (value - high.astype(jnp.float32)).astype(jnp.bfloat16)
    return high, low


def matmul(left, right):
    return jnp.dot(left, right, preferred_element_type=jnp.float32)


def put_across(ref, rows, value):
    width = value.shape[1]
    ref[rows, 0:width], ref[rows, width : 2 * width] = split(value)


def put_down(ref, row, depth, value, cols=slice(None)):
    count = value.shape[0]
    ref[row : row + count, cols], ref[depth + row : depth + row + count, cols] = split(value)


def across3(ref, rows, first, width, total):
    high = ref[rows, first : first + width]
    return jnp.concatenate([high, ref[rows, total + first : total + first + width], high], axis=1)


def table3(ref, cols=slice(None)):
    depth = ref.shape[0] // 2
    high = ref[0:depth, cols]
    return jnp.concatenate([high, high, ref[depth:, cols]], axis=0)


def data3(ref, first, depth, total, cols=slice(None)):
    high = ref[first : first + depth, cols]
    return jnp.concatenate([high, ref[total + first : total + first + depth, cols], high], axis=0)


def reverse(value):
    count = value.shape[0]
    i = lax.broadcasted_iota(jnp.int32, (count, count), 0)
    j = lax.broadcasted_iota(jnp.int32, (count, count), 1)
    swap = jnp.where(i + j == count - 1, 1.0, 0.0).astype(jnp.bfloat16)
    high, low = split(value)
    return matmul(swap, high) + matmul(swap, low)


def turn(value):
    return pltpu.roll(value, MARGIN, 1)


def low_lanes(rows):
    return lax.broadcasted_iota(jnp.int32, (rows, LANES), 1) < MARGIN


def window_rows(own_ref, left, right, rows):
    low = low_lanes(left.shape[0])
    one, two = turn(own_ref[rows, 0:LANES]), turn(own_ref[rows, LANES:TILE])
    return jnp.concatenate(
        [jnp.where(low, left, one), jnp.where(low, one, two), jnp.where(low, two, right)], axis=1
    )


def ends_kernel(row_ref, est_ref, obs_ref, left_ref, right_ref, pair_ref, outer_ref):
    even = lax.rem(row_ref[0], 2) == 0
    ends = []
    for est_first, obs_first in ((0, 0), (TILE - MARGIN, TILE - RADIUS)):
        rows = slice(est_first, est_first + MARGIN)
        top = window_rows(est_ref, left_ref[rows, :], right_ref[rows, :], rows)
        rows = slice(obs_first, obs_first + RADIUS)
        low = window_rows(obs_ref, turn(left_ref[rows, :]), turn(right_ref[rows, :]), rows)
        ends.append((top, low))
    for part, rows in ((0, slice(0, MARGIN)), (1, slice(MARGIN, HALO))):
        pair_ref[rows, :] = jnp.where(even, ends[1][part], ends[0][part])
        outer_ref[rows, :] = jnp.where(even, ends[0][part], ends[1][part])


def paired(top, low, near, far):
    a, b, c, d = top[:, near], top[:, far], low[:, near], low[:, far]
    return a - d, b + c, a + d, b - c


def analyse(fold_ref, first, count, col_in_ref, sums_ref):
    for block in range(2):
        cols = slice(block * BLOCK, (block + 1) * BLOCK)
        left = across3(fold_ref, slice(first, first + 2 * count), block * LANES, BLOCK, FRAME)
        put_down(sums_ref, 0, 2 * count, matmul(left, table3(col_in_ref, cols)), cols)


def spectrum(row_ref, sums_ref, count, spec_ref, add):
    for block in range(2):
        near = slice(block * BLOCK, block * BLOCK + LANES)
        far = slice(block * BLOCK + LANES, (block + 1) * BLOCK)
        cols = slice(block * BLOCK, (block + 1) * BLOCK)
        top = matmul(row_ref[0:HALF, :], data3(sums_ref, 0, count, 2 * count, cols))
        low = matmul(row_ref[HALF:FRAME, :], data3(sums_ref, count, count, 2 * count, cols))
        parts = paired(top, low, slice(0, LANES), slice(LANES, BLOCK))
        for part, rows, lanes in zip(
            parts,
            (slice(0, HALF), slice(0, HALF), slice(HALF, FRAME), slice(HALF, FRAME)),
            (near, far, near, far),
            strict=True,
        ):
            spec_ref[rows, lanes] = add[rows, lanes] + part if add is not None else part


def prepare_kernel(
    est_ref, obs_ref, left_ref, right_ref, bank_ref, table_ref,
    kern_ref, spec_ref, frame_ref,
    raw_ref, wide_ref, tall_ref, fold_ref, sums_ref,
):
    row_own_ref = table_ref.at[0:FRAME, BLOCK : BLOCK + 3 * LANES]
    col_in_ref = table_ref.at[FRAME : FRAME + 2 * BLOCK, 0 : 2 * BLOCK]
    kernel_cols_ref = table_ref.at[FRAME + 2 * BLOCK : FRAME + 3 * BLOCK, 0:BLOCK]
    left, right = (lambda rows: left_ref[rows, :]), (lambda rows: right_ref[rows, :])
    upper, under = slice(0, LANES), slice(LANES, TILE)
    top = window_rows(est_ref, left(upper), right(upper), upper)
    low = reverse(window_rows(est_ref, left(under), right(under), under))
    put_across(fold_ref, slice(0, LANES), top - low)
    put_across(fold_ref, slice(LANES, TILE), top + low)
    frame_ref[upper, :] = window_rows(obs_ref, turn(left(upper)), turn(right(upper)), upper)
    frame_ref[under, :] = reverse(window_rows(obs_ref, turn(left(under)), turn(right(under)), under))

    shape = (SIDE, SIDE)
    a = lax.broadcasted_iota(jnp.int32, shape, 0).astype(jnp.float32) - RADIUS
    b = lax.broadcasted_iota(jnp.int32, shape, 1).astype(jnp.float32) - RADIUS
    envelope = jnp.exp(-(a * a + b * b) / (2.0 * (0.625 * RADIUS) ** 2))
    raw_ref[...] = jnp.zeros_like(raw_ref)
    for model in range(MODELS):
        raw = bank_ref[:, model, :] * envelope
        total = jnp.sum(jnp.sum(raw, axis=1, keepdims=True), axis=0, keepdims=True)
        raw_ref[model * DEPTH : model * DEPTH + SIDE, 0:SIDE] = raw / total
    put_across(wide_ref, slice(None), raw_ref[...])
    part = matmul(across3(wide_ref, slice(None), 0, LANES, LANES), table3(kernel_cols_ref))
    for model in range(MODELS):
        put_down(tall_ref, 2 * DEPTH * model, DEPTH, part[model * DEPTH : (model + 1) * DEPTH, :])
    gain = 2.0 / (FRAME * BLOCK)
    for model in range(MODELS):
        right = data3(tall_ref, 2 * DEPTH * model, DEPTH, DEPTH)
        top = matmul(table_ref[0:HALF, 0 : 3 * DEPTH], right)
        low = matmul(table_ref[HALF:FRAME, 0 : 3 * DEPTH], right)
        parts = paired(top, low, slice(0, LANES), slice(LANES, BLOCK))
        kern_ref[model, 0:HALF, 0:LANES] = parts[0] * gain
        kern_ref[model, 0:HALF, LANES:BLOCK] = parts[1] * gain
        kern_ref[model, HALF:FRAME, 0:LANES] = parts[2] * gain
        kern_ref[model, HALF:FRAME, LANES:BLOCK] = parts[3] * gain

    analyse(fold_ref, 0, LANES, col_in_ref, sums_ref)
    spectrum(row_own_ref, sums_ref, LANES, spec_ref, None)


def product(spec_ref, kern, block, sign, grown, first, last):
    near = slice(block * BLOCK, block * BLOCK + LANES)
    far = slice(block * BLOCK + LANES, (block + 1) * BLOCK)
    top, low = slice(first, last), slice(HALF + first, HALF + last)
    out = []
    for rows in (top, low):
        fr, fi = spec_ref[rows, near], spec_ref[rows, far]
        kr, ki = kern[rows, 0:LANES], kern[rows, LANES:BLOCK]
        if sign > 0:
            out.append((fr * kr - fi * ki, fr * ki + fi * kr))
        else:
            out.append((fr * kr + fi * ki, fi * kr - fr * ki))
    (ur, ui), (vr, vi) = out
    cos_ref, sin_ref = grown
    put_down(cos_ref, first, HALF, ur + vr, slice(0, LANES))
    put_down(cos_ref, first, HALF, ui + vi, slice(LANES, BLOCK))
    put_down(sin_ref, first, HALF, ui - vi, slice(0, LANES))
    put_down(sin_ref, first, HALF, vr - ur, slice(LANES, BLOCK))


def maps_kernel(
    member_ref, row_ref, col_ref, index_ref, cover_ref, pick_ref, mask_ref, own_ref, odd_ref, weight_ref
):
    member, tile_row, tile_col = member_ref[0], row_ref[0], col_ref[0]
    rows_of_tiles, cols_of_tiles, exposures = cover_ref.shape
    lane = lax.broadcasted_iota(jnp.int32, (RADIUS, FRAME), 1)
    for step, spans in ((-1, ((LANES, RADIUS),)), (0, ((0, LANES), (FOLD, LANES))), (1, ((FOLD + LANES, RADIUS),))):
        near = []
        for side in (-1, 0, 1):
            r, c = tile_row + step, tile_col + side
            inside = (r >= 0) & (r < rows_of_tiles) & (c >= 0) & (c < cols_of_tiles)
            r = jnp.clip(r, 0, rows_of_tiles - 1)
            c = jnp.clip(c, 0, cols_of_tiles - 1)
            near.append((index_ref[c, r], jnp.where(inside, cover_ref[r, c, member], 0)))

        def spread(which, near=near):
            middle = jnp.where(lane < MARGIN + TILE, near[1][which], near[2][which])
            return jnp.where(lane < MARGIN, near[0][which], middle)

        pick = spread(0)
        cover = jnp.where((lane >= RADIUS) & (lane < FRAME - RADIUS), spread(1), 0)
        for first, count in spans:
            for row in range(first, first + count, RADIUS):
                pick_ref[row : row + RADIUS, :] = pick
                mask_ref[row : row + RADIUS, :] = cover

    covering = lax.fori_loop(0, exposures, lambda e, n: n + cover_ref[tile_row, tile_col, e], 0)
    own_cover = cover_ref[tile_row, tile_col, member].astype(jnp.float32)
    own_ref[...] = jnp.full(own_ref.shape, index_ref[tile_col, tile_row], jnp.int32)
    odd_ref[...] = jnp.full(odd_ref.shape, lax.rem(tile_row, 2), jnp.int32)
    weight_ref[...] = jnp.full(weight_ref.shape, own_cover, jnp.float32) / jnp.full(
        weight_ref.shape, covering.astype(jnp.float32), jnp.float32
    )


def update_kernel(
    pick_ref, mask_ref, own_ref, odd_ref, weight_ref,
    est_ref, frame_ref, pair_ref, outer_ref, kern_ref, part_ref,
    row_margin_ref, row_in_ref, row_out_ref, ready_ref, col_out_ref,
    out_ref,
    fold_ref, sums_ref, spec_ref, cos0_ref, sin0_ref, cos1_ref, sin1_ref, mid0_ref, mid1_ref,
    blur_ref, own_kern_ref, edge_ref,
):
    col_in_ref = ready_ref.at[FRAME : FRAME + 2 * BLOCK, 0 : 2 * BLOCK]
    grown = ((cos0_ref, sin0_ref), (cos1_ref, sin1_ref))
    mids = (mid0_ref, mid1_ref)

    odd = odd_ref[0:1, :] != 0
    above = jnp.where(odd, pair_ref[...], outer_ref[...])
    below = jnp.where(odd, outer_ref[...], pair_ref[...])
    top = above[0:MARGIN, :]
    low = reverse(below[0:MARGIN, :])
    put_across(fold_ref, slice(0, MARGIN), top - low)
    put_across(fold_ref, slice(MARGIN, 2 * MARGIN), top + low)
    analyse(fold_ref, 0, MARGIN, col_in_ref, sums_ref)
    spectrum(row_margin_ref, sums_ref, MARGIN, spec_ref, part_ref)

    own = own_ref[0:1, :]
    for row in range(0, FRAME, 48):
        rows = slice(row, row + 48)
        for lanes in (slice(0, LANES), slice(LANES, BLOCK)):
            chosen = kern_ref[0, rows, lanes]
            for model in range(1, MODELS):
                chosen = jnp.where(own == model, kern_ref[model, rows, lanes], chosen)
            own_kern_ref[rows, lanes] = chosen

    def rows_back(block, count, step=None):
        cos_ref, sin_ref = grown[block]
        even = matmul(row_out_ref[0:count, :], data3(cos_ref, 0, HALF, HALF))
        if step is not None:
            step(0)
        odd = matmul(row_out_ref[FOLD : FOLD + count, :], data3(sin_ref, 0, HALF, HALF))
        if step is not None:
            step(1)
        put_across(mids[block], slice(0, count), odd + even)
        put_across(mids[block], slice(count, 2 * count), odd - even)

    def grow(kern, block, sign):
        def step(part):
            for first in range(part * HALF // 2, (part + 1) * HALF // 2, 48):
                product(spec_ref, kern, block, sign, grown[block], first, first + 48)

        return step

    def columns_back(block):
        return matmul(
            across3(mids[block], slice(0, REACH), 0, BLOCK, BLOCK),
            table3(col_out_ref, slice(block * BLOCK, (block + 1) * BLOCK)),
        )

    def keep(lanes, value, model):
        blur_ref[:, lanes] = jnp.where(pick_ref[:, lanes] == model, value, blur_ref[:, lanes])

    def forward(model):
        rows_back(0, FOLD, grow(kern_ref.at[model], 1, 1))
        one = columns_back(0)
        keep(slice(0, LANES), one[:, 0:LANES], model)
        edge_ref[...] = one[:, LANES:BLOCK]
        rows_back(1, FOLD, grow(kern_ref.at[model + 1], 0, 1) if model + 1 < MODELS else None)
        two = columns_back(1)
        keep(slice(LANES, BLOCK), edge_ref[...] + two[:, 0:LANES], model)
        keep(slice(BLOCK, FRAME), two[:, LANES:BLOCK], model)

    grow(kern_ref.at[0], 0, 1)(0)
    grow(kern_ref.at[0], 0, 1)(1)
    for model in range(MODELS):
        forward(model)

    def ratio(rows, values):
        return jnp.where(mask_ref[rows, :] != 0, values / blur_ref[rows, :], 0.0)

    spare = jnp.zeros((RADIUS, 2 * FRAME), jnp.bfloat16)
    fold_ref[FOLD:HALF, :] = spare
    fold_ref[HALF + FOLD : FRAME, :] = spare
    for row in range(0, LANES, 64):
        top = ratio(slice(row, row + 64), frame_ref[row : row + 64, :])
        low = ratio(slice(FOLD + row, FOLD + row + 64), frame_ref[LANES + row : LANES + row + 64, :])
        put_across(fold_ref, slice(row, row + 64), top - low)
        put_across(fold_ref, slice(HALF + row, HALF + row + 64), top + low)
    top = ratio(slice(LANES, FOLD), above[MARGIN:HALO, :])
    low = ratio(slice(FOLD + LANES, REACH), reverse(below[MARGIN:HALO, :]))
    put_across(fold_ref, slice(LANES, FOLD), top - low)
    put_across(fold_ref, slice(HALF + LANES, HALF + FOLD), top + low)
    analyse(fold_ref, 0, HALF, col_in_ref, sums_ref)
    spectrum(row_in_ref, sums_ref, HALF, spec_ref, None)

    weight = weight_ref[0:1, :]
    grow(own_kern_ref, 0, -1)(0)
    grow(own_kern_ref, 0, -1)(1)
    rows_back(0, LANES, grow(own_kern_ref, 1, -1))
    rows_back(1, LANES)
    for block in range(2):
        own = slice(block * LANES, (block + 1) * LANES)
        back = matmul(across3(mids[block], slice(0, TILE), 0, BLOCK, BLOCK), table3(col_out_ref, slice(block * BLOCK + MARGIN, block * BLOCK + MARGIN + LANES))) * weight
        out_ref[0:LANES, own] = est_ref[0:LANES, own] * back[0:LANES, :]
        out_ref[LANES:TILE, own] = est_ref[LANES:TILE, own] * reverse(back[LANES:TILE, :])


VMEM = pl.BlockSpec(memory_space=pltpu.VMEM)
SMEM = pl.BlockSpec(memory_space=pltpu.SMEM)


def f32(*shape):
    return jax.ShapeDtypeStruct(shape, jnp.float32)


def half_scratch(*shape):
    return pltpu.VMEM(shape, jnp.bfloat16)


def pack_ends(row, estimate, frame, left, right):
    return pl.pallas_call(
        ends_kernel,
        out_shape=(f32(HALO, FRAME),) * 2,
        in_specs=[SMEM] + [VMEM] * 4,
        out_specs=(VMEM,) * 2,
        compiler_params=pltpu.CompilerParams(vmem_limit_bytes=4 << 20),
        name="pack_ends",
    )(row, estimate, frame, left, right)


def pixel_maps(member, row, col, index, coverage):
    whole = jax.ShapeDtypeStruct((REACH, FRAME), jnp.int32)
    small = (8, LANES)
    return pl.pallas_call(
        maps_kernel,
        out_shape=(
            whole, whole, jax.ShapeDtypeStruct(small, jnp.int32),
            jax.ShapeDtypeStruct((8, FRAME), jnp.int32), f32(*small),
        ),
        in_specs=[SMEM] * 5,
        out_specs=(VMEM,) * 5,
        compiler_params=pltpu.CompilerParams(vmem_limit_bytes=4 << 20),
        cost_estimate=pl.CostEstimate(flops=1 << 28, bytes_accessed=1 << 20, transcendentals=0),
        name="pixel_maps",
    )(member, row, col, index, coverage)


def prepare(estimate, frame, left, right, bank, table):
    return pl.pallas_call(
        prepare_kernel,
        out_shape=(f32(MODELS, FRAME, BLOCK), f32(FRAME, 2 * BLOCK), f32(TILE, FRAME)),
        in_specs=[VMEM] * 6,
        out_specs=(VMEM,) * 3,
        scratch_shapes=[
            pltpu.VMEM((MODELS * DEPTH, LANES), jnp.float32),
            half_scratch(MODELS * DEPTH, 2 * LANES),
            half_scratch(MODELS * 2 * DEPTH, BLOCK),
            half_scratch(TILE, 2 * FRAME),
            half_scratch(2 * TILE, 2 * BLOCK),
        ],
        compiler_params=pltpu.CompilerParams(vmem_limit_bytes=16 << 20),
        cost_estimate=pl.CostEstimate(flops=2 << 30, bytes_accessed=4 << 20, transcendentals=8192),
        name="prepare",
    )(estimate, frame, left, right, bank, table["ready"])


def tile_update(maps, estimate, frame, pair, outer, spectra, part, table):
    names = ("row_margin", "row_in", "row_out", "ready", "col_out")
    return pl.pallas_call(
        update_kernel,
        out_shape=f32(TILE, TILE),
        in_specs=[VMEM] * 16,
        out_specs=VMEM,
        scratch_shapes=[
            half_scratch(FRAME, 2 * FRAME),
            half_scratch(2 * FRAME, 2 * BLOCK),
            pltpu.VMEM((FRAME, 2 * BLOCK), jnp.float32),
            half_scratch(FRAME, BLOCK),
            half_scratch(FRAME, BLOCK),
            half_scratch(FRAME, BLOCK),
            half_scratch(FRAME, BLOCK),
            half_scratch(REACH, 2 * BLOCK),
            half_scratch(REACH, 2 * BLOCK),
            pltpu.VMEM((REACH, FRAME), jnp.float32),
            pltpu.VMEM((FRAME, BLOCK), jnp.float32),
            pltpu.VMEM((REACH, LANES), jnp.float32),
        ],
        compiler_params=pltpu.CompilerParams(vmem_limit_bytes=20 << 20),
        cost_estimate=pl.CostEstimate(flops=4 << 30, bytes_accessed=8 << 20, transcendentals=0),
        name="tile_update",
    )(
        *maps, estimate, frame, pair, outer, spectra, part,
        *(table[name] for name in names),
    )


def exchange(first, last, axis):
    upward = [(i, i + 1) for i in range(lax.axis_size(axis) - 1)]
    after = lax.ppermute(first, axis, [(b, a) for a, b in upward])
    return lax.ppermute(last, axis, upward), after


def trade(pair, outer, axis):
    count = lax.axis_size(axis)
    swap = lambda first: [
        step for i in range(first, count - 1, 2) for step in ((i, i + 1), (i + 1, i))
    ]
    return lax.ppermute(pair, axis, swap(0)), lax.ppermute(outer, axis, swap(1))


def exposure_sum(block):
    rows, cols = block.shape
    near = lax.axis_size("exp_y")
    pieces = lax.all_to_all(block.reshape(near, rows // near, cols), "exp_y", 0, 0)
    piece = jnp.sum(pieces, axis=0)
    piece = piece + lax.ppermute(piece, "exp_z", [(0, 1), (1, 0)])
    spread = jnp.broadcast_to(piece[None], (near,) + piece.shape)
    return lax.all_to_all(spread, "exp_y", 0, 0).reshape(rows, cols)


def shards(estimate, observed, psf_bank, psf_index, coverage):
    table = {name: jnp.asarray(value) for name, value in tables().items()}
    frame = observed[0]
    member, row, col = (
        lax.axis_index(axis).astype(jnp.int32).reshape(1)
        for axis in (("exp_y", "exp_z"), "skyx", "skyy")
    )
    bank = psf_bank[0].transpose(1, 0, 2)
    index = psf_index[0].transpose(1, 0)
    cover = coverage.transpose(1, 2, 0)
    own = estimate
    first = jnp.concatenate([frame[:, :MARGIN], own[:, :MARGIN]], axis=1)
    last = jnp.concatenate([own[:, TILE - MARGIN :], frame[:, TILE - MARGIN :]], axis=1)
    sides = exchange(first, last, "skyy")
    maps = pixel_maps(member, row, col, index, cover)
    ends = trade(*pack_ends(row, own, frame, *sides), "skyx")
    spectra, part, folded = prepare(own, frame, *sides, bank, table)
    update = tile_update(maps, own, folded, *ends, spectra, part, table)
    return exposure_sum(update)


def solution(mesh):
    exp_count, sky_rows, sky_cols = mesh.devices.shape
    mesh = Mesh(
        mesh.devices.reshape(exp_count // 2, 2, sky_rows, sky_cols),
        ("exp_y", "exp_z", "skyx", "skyy"),
    )
    exp = ("exp_y", "exp_z")
    in_specs = (
        P("skyx", "skyy"),
        P(exp, "skyx", "skyy"),
        P(exp, None, None, None),
        P(exp, None, None),
        P(),
    )
    return jax.shard_map(
        shards, mesh=mesh, in_specs=in_specs, out_specs=P("skyx", "skyy"), check_vma=False
    )
```
